128 devices in a mesh: win: 4 (over y_lo, core), srow: 4 (over x), scol: 8 (over z, y_hi).
Axes of the slice: x: 4, y: 4 (y_hi: 2, y_lo: 2; y = y_hi * 2 + y_lo), z: 4, core: 2. Of those that a mesh axis runs over, the one named last changes fastest.
Arguments:
- spectra: float32 [4, 2, 64, 4096], P(None, None, 'win', ('srow', 'scol')), may hold values from -6 to 6
- bins: int32 [4], replicated, may hold values from 1 to 2047
- travel: int32 [4096, 2048], P(('srow', 'scol'), 'win'), may hold values from 0 to 16383
Outputs:
- coherence: bfloat16 [4, 2, 4096, 4, 1024], P('win', None, 'srow', None, 'scol')
- beam: float32 [4, 2048], P('win')
The draws below stay inside these ranges and needn't reach their ends.
All inputs are finite; a program needn't handle non-finite values.
Results may differ from the reference program's by a relative error of at most 0.012.
Values may be sent and summed in bfloat16 or wider, within the bound.
No kernel may reach another device: no remote copies, remote signals or barrier semaphores. Data moves between devices by JAX's collectives and lax.ppermute only.
A program may use at most 128 MiB of HBM per device.

```python
import math
import jax
import jax.numpy as jnp
from jax import lax

S = 4096
F = 4
P_SIZE = 2048
NFFT = 4096
TMAX = 16384
W = 64
BLOCK = 1024


def plant(result, stream_key, low, top_value):
    longest = result.shape.index(max(result.shape))
    spots = []
    for shift in (0, 1):
        where = [jax.random.randint(jax.random.fold_in(stream_key, axis), (), 0, length) for axis, length in enumerate(result.shape)]
        where[longest] = (where[longest] + shift) % result.shape[longest]
        spots.append(tuple(where))
    return result.at[spots[0]].set(low).at[spots[1]].set(top_value)


def steps_of(rng, dims, cuts, low, high):
    factor_of = 1.0
    for dim, parts in cuts:
        steps = jax.random.uniform(jax.random.fold_in(jax.random.fold_in(rng, 6), dim), (parts,), jnp.float32, low / len(cuts), high / len(cuts))
        factor_of = factor_of * jnp.repeat(jnp.exp(steps), dims[dim] // parts).reshape((-1,) + (1,) * (len(dims) - 1 - dim))
    return factor_of


def gaussian(rng, shape, scale, bound, pieces=(), dtype=jnp.bfloat16):
    level = steps_of(rng, shape, pieces, -0.22, 0.18) if pieces else 1.0
    entries = jax.random.normal(rng, shape, jnp.float32) * scale * level
    return jnp.minimum(jnp.maximum(entries, -bound), bound).astype(dtype)


def setup_inputs(seed: int = 0) -> dict:
    key_list = jax.random.split(jax.random.key(seed), 4)
    spectra = gaussian(key_list[0], (F, 2, W, S), 1.0, 6.0, ((2, 4), (3, 32)), jnp.float32)
    bins = plant(jax.random.randint(key_list[1], (F,), 1, NFFT // 2), jax.random.fold_in(key_list[1], 1), 1, (NFFT // 2) - 1).astype(jnp.int32)
    travel = plant(jax.random.randint(key_list[2], (S, P_SIZE), 0, TMAX), jax.random.fold_in(key_list[2], 1), 0, TMAX - 1).astype(jnp.int32)
    return dict(spectra=spectra, bins=bins, travel=travel)


def reference(spectra, bins, travel):
    magnitude = jnp.sqrt(spectra[:, 0] * spectra[:, 0] + spectra[:, 1] * spectra[:, 1] + 0.5)
    normal = (spectra / magnitude[:, None]).astype(jnp.bfloat16).astype(jnp.float32)
    highest = lax.Precision.HIGHEST

    def one_freq(inputs):
        piece, bin_index = inputs
        real = jnp.dot(piece[0].T, piece[0], precision=highest) + jnp.dot(piece[1].T, piece[1], precision=highest)
        imag = jnp.dot(piece[1].T, piece[0], precision=highest) - jnp.dot(piece[0].T, piece[1], precision=highest)
        extent = jnp.sqrt(real * real + imag * imag + float(W))
        coh_real = (real / extent).astype(jnp.bfloat16)
        coh_imag = (imag / extent).astype(jnp.bfloat16)
        cycles = bin_index * travel % NFFT
        angle = 2.0 * math.pi / NFFT * cycles.astype(jnp.float32)
        steer_real = jnp.cos(angle).astype(jnp.bfloat16).astype(jnp.float32)
        steer_imag = (-jnp.sin(angle)).astype(jnp.bfloat16).astype(jnp.float32)
        kreal = coh_real.astype(jnp.float32)
        kimag = coh_imag.astype(jnp.float32)
        image_real = jnp.dot(kreal, steer_real, precision=highest) - jnp.dot(kimag, steer_imag, precision=highest)
        image_imag = jnp.dot(kreal, steer_imag, precision=highest) + jnp.dot(kimag, steer_real, precision=highest)
        power = lax.optimization_barrier(jnp.sum(steer_real * image_real + steer_imag * image_imag, axis=0)) / S
        stacked = jnp.stack([coh_real, coh_imag]).reshape(2, S, S // BLOCK, BLOCK)
        return (stacked, power)
    coherence, beam = lax.map(one_freq, (normal, bins))
    return (coherence, beam)
```

```python
import jax
import jax.numpy as jnp
from jax import lax
from jax.experimental import pallas as pl
from jax.experimental.pallas import tpu as pltpu
from jax.sharding import PartitionSpec as P

S = 4096
NFFT = 4096
F = 4
NST = 128
NPT = 512
ALL = ("win", "srow", "scol")
ROW_OFF = (0, 1, 2, -3, 4)
ROW_WEIGHT = (1.0, 2.0, 2.0, 2.0, 1.0)
EXTRA_OFF = (-1, -2, 3)
ROUND = 12582912.0

ROOT2 = 2.0**0.5
SIN = [ROOT2 * v for v in (3.141592580044453, -5.167706878911761, 2.5500313770692338,
                           -0.5980451729935192, 0.07722012694435497)]
COS = [-ROOT2 * v for v in (0.9999999534664096, -4.93479285864205, 4.058411913501759,
                            -1.331880156986464, 0.2196967900729894)]


def prep_kernel(spectra, travel, payload, pieces):
    payload[0:NST, :] = travel[...].astype(jnp.int16)
    for f in range(F):
        re = spectra[f, 0]
        im = spectra[f, 1]
        magnitude = jnp.sqrt(re * re + im * im + 0.5)
        for c, part in enumerate((re, im)):
            value = (part / magnitude).astype(jnp.bfloat16).astype(jnp.float32) * 32768.0
            value = jnp.clip((value + ROUND) - ROUND, -32767.0, 32767.0)
            code = value.astype(jnp.int32).astype(jnp.int16)
            lanes = slice(f * NST, (f + 1) * NST)
            payload[NST + 16 * c:NST + 16 * (c + 1), lanes] = code
            pieces[16 * c:16 * (c + 1), lanes] = code


def steer_kernel(bins, *refs):
    payloads, out = refs[:-1], refs[-1]
    rows = 16
    for n, ref in enumerate(payloads):
        def chunk(i, carry, n=n, ref=ref):
            at = pl.ds(pl.multiple_of(i * rows, rows), rows)
            samples = (ref[at, :].astype(jnp.int32) & (NFFT - 1)).astype(jnp.float32)
            for f in range(F):
                scale = bins[f].astype(jnp.float32) * (1.0 / NFFT)
                turns = samples * scale
                r = turns - ((turns + ROUND) - ROUND)
                z = r * r
                s = SIN[4]
                c = COS[4]
                for k in (3, 2, 1, 0):
                    s = s * z + SIN[k]
                    c = c * z + COS[k]
                s = s * r
                out[f, 0, n, at, :] = (1.0 - s * s).astype(jnp.bfloat16)
                out[f, 1, n, at, :] = (s * c).astype(jnp.bfloat16)
            return carry

        lax.fori_loop(0, NST // rows, chunk, 0)


def steer(bins, payloads):
    n = len(payloads)
    return pl.pallas_call(
        steer_kernel,
        out_shape=jax.ShapeDtypeStruct((F, 2, n, NST, NPT), jnp.bfloat16),
        in_specs=[pl.BlockSpec(memory_space=pltpu.SMEM)]
        + [pl.BlockSpec(memory_space=pltpu.VMEM)] * n,
        name="steer%d" % n,
    )(bins, *payloads)


def beam_kernel(place, own_steer, far_steer, a0, a1, a2, a3, coherence, beam, scratch):
    f = pl.program_id(0)
    w, r, c = place[0], place[1], place[2]
    sources = (a0, a1, a2, a3)

    def pieces(block):
        return [
            (a[block].astype(jnp.int32).astype(jnp.float32) * (1.0 / 32768.0)).astype(jnp.bfloat16)
            for a in sources
        ]

    cols = [pieces(n) for n in range(4)]
    x_cols = jnp.concatenate([jnp.concatenate(p, axis=0) for p in cols], axis=1)
    y_cols = jnp.concatenate(
        [jnp.concatenate([q for v in p for q in (-v[16:32], v[0:16])], axis=0) for p in cols], axis=1
    )
    steer_cols = jnp.concatenate(
        [ref for part in range(2) for ref in (own_steer[0, part, 0], *(far_steer[0, part, n] for n in range(3)))],
        axis=0,
    )

    def cross(block):
        x = cols[0] if block == 0 else pieces(block)
        x = jnp.concatenate(x, axis=0)
        dims = (((0,), (0,)), ((), ()))
        re = lax.dot_general(x, x_cols, dims, preferred_element_type=jnp.float32)
        im = lax.dot_general(x, y_cols, dims, preferred_element_type=jnp.float32)
        inverse = lax.rsqrt(re * re + im * im + 64.0)
        return re * inverse, im * inverse

    def keep(parts, offset):
        row = (c + offset) & 7
        at = pl.ds(pl.multiple_of(row * (4 * NST), 4 * NST), 4 * NST)
        for part in range(2):
            for d in range(4):
                b = (r + d) & 3
                scratch[pl.ds(b, NST, stride=4), :] = parts[part][:, d * NST:(d + 1) * NST]
            coherence[part, at, :] = scratch[...].astype(jnp.bfloat16)

    total = jnp.zeros((8, NPT), jnp.float32)
    for k, (offset, weight) in enumerate(zip(ROW_OFF, ROW_WEIGHT)):
        re, im = cross(0 if k == 0 else 3 + k)

        @pl.when(f == w)
        def _():
            keep((re, im), offset)

        re = re.astype(jnp.bfloat16)
        im = im.astype(jnp.bfloat16)
        left = jnp.concatenate(
            [jnp.concatenate([re, -im], axis=1), jnp.concatenate([im, re], axis=1)], axis=0
        )
        image = jnp.dot(left, steer_cols, preferred_element_type=jnp.float32)
        if k == 0:
            row_re, row_im = own_steer[0, 0, 0], own_steer[0, 1, 0]
        else:
            row_re, row_im = far_steer[0, 0, 2 + k], far_steer[0, 1, 2 + k]
        power = row_re.astype(jnp.float32) * image[:NST] + row_im.astype(jnp.float32) * image[NST:]
        power = power.reshape(NST // 8, 8, NPT).sum(axis=0)
        total = total + (power if weight == 1.0 else weight * power)

    @pl.when(f == w)
    def _():
        for n, offset in enumerate(EXTRA_OFF):
            keep(cross(8 + n), offset)

    value = jnp.sum(total, axis=0, keepdims=True) * (1.0 / S)
    for j in range(4):
        beam[0, :, j, :] = jnp.broadcast_to(value[:, j * NST:(j + 1) * NST], (32, NST))


def beams(place, own_steer, far_steer, spectra):
    blocks = spectra[0].shape[0]
    piece = pl.BlockSpec((blocks, 32, NST), lambda f: (0, 0, f))
    return pl.pallas_call(
        beam_kernel,
        grid=(F,),
        out_shape=(
            jax.ShapeDtypeStruct((2, 4 * 1024, NST), jnp.bfloat16),
            jax.ShapeDtypeStruct((F, 32, 4, NST), jnp.float32),
        ),
        in_specs=[
            pl.BlockSpec(memory_space=pltpu.SMEM),
            pl.BlockSpec((1, 2, 1, NST, NPT), lambda f: (f, 0, 0, 0, 0)),
            pl.BlockSpec((1, 2, 7, NST, NPT), lambda f: (f, 0, 0, 0, 0)),
            piece, piece, piece, piece,
        ],
        out_specs=(
            pl.BlockSpec((2, 4 * 1024, NST), lambda f: (0, 0, 0)),
            pl.BlockSpec((1, 32, 4, NST), lambda f: (f, 0, 0, 0)),
        ),
        scratch_shapes=[pltpu.VMEM((4 * NST, NST), jnp.float32)],
        name="beams",
    )(place, own_steer, far_steer, *spectra)


def from_offset(value, axis, offset):
    size = lax.axis_size(axis)
    return lax.ppermute(value, axis, [((i + offset) % size, i) for i in range(size)])


def from_partner(value, bit):
    return lax.ppermute(value, "win", [(i ^ bit, i) for i in range(4)])


def body(spectra, bins, travel):
    payload, own_pieces = pl.pallas_call(
        prep_kernel,
        out_shape=(
            jax.ShapeDtypeStruct((NST + 32, NPT), jnp.int16),
            jax.ShapeDtypeStruct((32, NPT), jnp.int16),
        ),
        name="prep",
    )(spectra, travel)
    far = [from_offset(payload, "srow", d) for d in (1, 2, 3)]
    far += [from_offset(payload, "scol", d) for d in ROW_OFF[1:]]
    extra = [from_offset(own_pieces, "scol", d) for d in EXTRA_OFF]
    own_steer = steer(bins, [payload])
    far_steer = steer(bins, far)
    a0 = jnp.stack([own_pieces] + [v[NST:] for v in far] + extra)
    a1 = from_partner(a0, 2)
    a2 = from_partner(a0, 1)
    a3 = from_partner(a1, 1)
    place = jnp.stack([lax.axis_index(a) for a in ALL]).astype(jnp.int32)
    coherence, partial = beams(place, own_steer, far_steer, (a0, a1, a2, a3))
    shares = lax.all_to_all(partial.reshape(128, 4, NST), ALL, 0, 0, tiled=True)
    beam = shares.reshape(4, 32, 4, NST).sum(axis=1).reshape(1, 4 * NPT)
    return coherence.reshape(1, 2, 1024, 4, NST), beam


def solution(mesh):
    placed = (P(None, None, "win", ("srow", "scol")), P(), P(("srow", "scol"), "win"))
    return jax.shard_map(
        body,
        mesh=mesh,
        in_specs=placed,
        out_specs=(P("win", None, "srow", None, "scol"), P("win", None)),
        check_vma=False,
    )
```

```python
import jax
import jax.numpy as jnp
from jax import lax
from jax.experimental import pallas as pl
from jax.experimental.pallas import tpu as pltpu
from jax.sharding import PartitionSpec as P

S = 4096
NFFT = 4096
F = 4
NST = 128
NPT = 512
ALL = ("win", "srow", "scol")
ROW_OFF = (0, 1, 2, -3, 4)
ROW_WEIGHT = (1.0, 2.0, 2.0, 2.0, 1.0)
RELAY = (4, 6, 7)
ROUND = 12582912.0
STEP = 32

ROOT2 = 2.0**0.5
SIN = [ROOT2 * v for v in (3.141592580044453, -5.167706878911761, 2.5500313770692338,
                           -0.5980451729935192, 0.07722012694435497)]
COS = [-ROOT2 * v for v in (0.9999999534664096, -4.93479285864205, 4.058411913501759,
                            -1.331880156986464, 0.2196967900729894)]


def prep_kernel(spectra, travel, payload):
    payload[0:NST, :] = travel[...].astype(jnp.int16)
    for f in range(F):
        re = spectra[f, 0]
        im = spectra[f, 1]
        magnitude = jnp.sqrt(re * re + im * im + 0.5)
        for c, part in enumerate((re, im)):
            value = (part / magnitude).astype(jnp.bfloat16).astype(jnp.float32) * 32768.0
            value = jnp.clip((value + ROUND) - ROUND, -32767.0, 32767.0)
            code = value.astype(jnp.int32).astype(jnp.int16)
            lanes = slice(f * NST, (f + 1) * NST)
            payload[NST + 16 * c:NST + 16 * (c + 1), lanes] = code


def steer_kernel(bins, *refs):
    payloads, out = refs[:-1], refs[-1]
    rows = 16
    for n, ref in enumerate(payloads):
        def chunk(i, carry, n=n, ref=ref):
            at = pl.ds(pl.multiple_of(i * rows, rows), rows)
            samples = (ref[at, :].astype(jnp.int32) & (NFFT - 1)).astype(jnp.float32)
            for f in range(F):
                scale = bins[f].astype(jnp.float32) * (1.0 / NFFT)
                turns = samples * scale
                r = turns - ((turns + ROUND) - ROUND)
                z = r * r
                s = SIN[4]
                c = COS[4]
                for k in (3, 2, 1, 0):
                    s = s * z + SIN[k]
                    c = c * z + COS[k]
                s = s * r
                out[f, 0, n, at, :] = (1.0 - s * s).astype(jnp.bfloat16)
                out[f, 1, n, at, :] = (s * c).astype(jnp.bfloat16)
            return carry

        lax.fori_loop(0, STEP // rows, chunk, 0)


def steer(bins, payloads):
    n = len(payloads)
    return pl.pallas_call(
        steer_kernel,
        grid=(NST // STEP,),
        out_shape=jax.ShapeDtypeStruct((F, 2, n, NST, NPT), jnp.bfloat16),
        in_specs=[pl.BlockSpec(memory_space=pltpu.SMEM)]
        + [pl.BlockSpec((STEP, NPT), lambda i: (i, 0))] * n,
        out_specs=pl.BlockSpec((F, 2, n, STEP, NPT), lambda i: (0, 0, 0, i, 0)),
        name="steer%d" % n,
    )(bins, *payloads)


def decode(sources, block):
    return [
        (a[block].astype(jnp.int32).astype(jnp.float32) * (1.0 / 32768.0)).astype(jnp.bfloat16)
        for a in sources
    ]


def columns(cols):
    x = jnp.concatenate([jnp.concatenate(p, axis=0) for p in cols], axis=1)
    y = jnp.concatenate(
        [jnp.concatenate([q for v in p for q in (-v[16:32], v[0:16])], axis=0) for p in cols], axis=1
    )
    return x, y


def coherent(row, x_cols, y_cols):
    x = jnp.concatenate(row, axis=0)
    dims = (((0,), (0,)), ((), ()))
    re = lax.dot_general(x, x_cols, dims, preferred_element_type=jnp.float32)
    im = lax.dot_general(x, y_cols, dims, preferred_element_type=jnp.float32)
    inverse = lax.rsqrt(re * re + im * im + 64.0)
    return re * inverse, im * inverse


def interleave(part, r, scratch):
    for d in range(4):
        scratch[pl.ds((r + d) & 3, NST, stride=4), :] = part[:, d * NST:(d + 1) * NST]
    return scratch[...].astype(jnp.bfloat16)


def beam_kernel(place, own_steer, col_steer, row_steer, a0, a1, a2, a3, coherence, beam, scratch):
    f = pl.program_id(0)
    w, r, c = place[0], place[1], place[2]
    sources = (a0, a1, a2, a3)

    cols = [decode(sources, n) for n in range(4)]
    x_cols, y_cols = columns(cols)
    steer_cols = jnp.concatenate(
        [ref for part in range(2) for ref in (own_steer[0, part, 0], *(row_steer[0, part, n] for n in range(3)))],
        axis=0,
    )

    total = jnp.zeros((8, NPT), jnp.float32)
    for k, (offset, weight) in enumerate(zip(ROW_OFF, ROW_WEIGHT)):
        re, im = coherent(cols[0] if k == 0 else decode(sources, 3 + k), x_cols, y_cols)

        @pl.when(f == w)
        def _():
            at = pl.ds(pl.multiple_of(((c + offset) & 7) * (4 * NST), 4 * NST), 4 * NST)
            coherence[0, at, :] = interleave(re, r, scratch)
            coherence[1, at, :] = interleave(im, r, scratch)

        re = re.astype(jnp.bfloat16)
        im = im.astype(jnp.bfloat16)
        left = jnp.concatenate(
            [jnp.concatenate([re, -im], axis=1), jnp.concatenate([im, re], axis=1)], axis=0
        )
        image = jnp.dot(left, steer_cols, preferred_element_type=jnp.float32)
        if k == 0:
            row_re, row_im = own_steer[0, 0, 0], own_steer[0, 1, 0]
        else:
            row_re, row_im = col_steer[0, 0, k - 1], col_steer[0, 1, k - 1]
        power = row_re.astype(jnp.float32) * image[:NST] + row_im.astype(jnp.float32) * image[NST:]
        power = power.reshape(NST // 8, 8, NPT).sum(axis=0)
        total = total + (power if weight == 1.0 else weight * power)

    value = jnp.sum(total, axis=0, keepdims=True) * (1.0 / S)
    for j in range(4):
        beam[0, :, j, :] = jnp.broadcast_to(value[:, j * NST:(j + 1) * NST], (32, NST))


def beams(place, own_steer, col_steer, row_steer, spectra):
    blocks = spectra[0].shape[0]
    piece = pl.BlockSpec((blocks, 32, NST), lambda f: (0, 0, f))
    return pl.pallas_call(
        beam_kernel,
        grid=(F,),
        out_shape=(
            jax.ShapeDtypeStruct((2, 4 * 1024, NST), jnp.bfloat16),
            jax.ShapeDtypeStruct((F, 32, 4, NST), jnp.float32),
        ),
        in_specs=[
            pl.BlockSpec(memory_space=pltpu.SMEM),
            pl.BlockSpec((1, 2, 1, NST, NPT), lambda f: (f, 0, 0, 0, 0)),
            pl.BlockSpec((1, 2, 4, NST, NPT), lambda f: (f, 0, 0, 0, 0)),
            pl.BlockSpec((1, 2, 3, NST, NPT), lambda f: (f, 0, 0, 0, 0)),
            piece, piece, piece, piece,
        ],
        out_specs=(
            pl.BlockSpec((2, 4 * 1024, NST), lambda f: (0, 0, 0)),
            pl.BlockSpec((1, 32, 4, NST), lambda f: (f, 0, 0, 0)),
        ),
        scratch_shapes=[pltpu.VMEM((4 * NST, NST), jnp.float32)],
        name="beams",
    )(place, own_steer, col_steer, row_steer, *spectra)


def rest_kernel(place, rows, a0, a1, a2, a3, old, coherence, scratch):
    x_cols, y_cols = columns([decode((a0, a1, a2, a3), n) for n in range(4)])
    re, im = coherent(decode([rows.at[k] for k in range(4)], 0), x_cols, y_cols)
    coherence[0] = interleave(re, place[1], scratch)
    coherence[1] = interleave(im, place[1], scratch)


def rest(place, rows, spectra, coherence):
    cols = pl.BlockSpec((4, 32, NST), lambda n, place: (0, 0, place[0]))
    at = lambda n, place: (0, (place[2] + 3 - 4 * n + 3 * (n // 2)) & 7, 0)
    return pl.pallas_call(
        rest_kernel,
        grid_spec=pltpu.PrefetchScalarGridSpec(
            num_scalar_prefetch=1,
            grid=(len(RELAY),),
            in_specs=[
                pl.BlockSpec((4, 1, 32, NST), lambda n, place: (0, n, 0, 0)),
                cols, cols, cols, cols,
                pl.BlockSpec(memory_space=pl.ANY),
            ],
            out_specs=pl.BlockSpec((2, 4 * NST, NST), at),
            scratch_shapes=[pltpu.VMEM((4 * NST, NST), jnp.float32)],
        ),
        out_shape=jax.ShapeDtypeStruct(coherence.shape, coherence.dtype),
        input_output_aliases={6: 0},
        name="rest",
    )(place, rows, *spectra, coherence)


def from_offset(value, axis, offset):
    size = lax.axis_size(axis)
    return lax.ppermute(value, axis, [((i + offset) % size, i) for i in range(size)])


def from_partner(value, bit):
    return lax.ppermute(value, "win", [(i ^ bit, i) for i in range(4)])


def body(spectra, bins, travel):
    payload = pl.pallas_call(
        prep_kernel,
        out_shape=jax.ShapeDtypeStruct((NST + 32, NPT), jnp.int16),
        name="prep",
    )(spectra, travel)
    place = jnp.stack([lax.axis_index(a) for a in ALL]).astype(jnp.int32)
    by_row = [from_offset(payload, "srow", d) for d in (1, 2, 3)]
    by_col = [from_offset(payload, "scol", d) for d in ROW_OFF[1:]]
    steer0 = steer(bins, [payload])
    a0 = jnp.stack([v[NST:] for v in [payload] + by_row + by_col])
    a1 = from_partner(a0, 2)
    a2 = from_partner(a0, 1)
    steer1 = steer(bins, by_col)
    a1, steer1 = lax.optimization_barrier((a1, steer1))
    a3 = from_partner(a1, 1)
    steer2 = steer(bins, by_row)
    sources = (a0, a1, a2, a3)
    own = [lax.dynamic_slice(a, (0, 0, NST * place[0]), (8, 32, NST)) for a in sources]
    rows = from_offset(jnp.stack([v[n] for v in own for n in RELAY]).reshape(4, 3, 32, NST), "scol", 2)
    coherence, partial = beams(place, steer0, steer1, steer2, sources)
    coherence = rest(place, rows, sources, coherence)
    shares = lax.all_to_all(partial.reshape(128, 4, NST), ALL, 0, 0, tiled=True)
    beam = shares.reshape(4, 32, 4, NST).sum(axis=1).reshape(1, 4 * NPT)
    return coherence.reshape(1, 2, 1024, 4, NST), beam


def solution(mesh):
    placed = (P(None, None, "win", ("srow", "scol")), P(), P(("srow", "scol"), "win"))
    return jax.shard_map(
        body,
        mesh=mesh,
        in_specs=placed,
        out_specs=(P("win", None, "srow", None, "scol"), P("win", None)),
        check_vma=False,
    )
```

```python
import jax
import jax.numpy as jnp
from jax import lax
from jax.experimental import pallas as pl
from jax.experimental.pallas import tpu as pltpu
from jax.sharding import PartitionSpec as P


S = 4096
NFFT = 4096
F = 4
NST = 128
NPT = 512
ALL = ("win", "srow", "scol")
ROW_OFF = (0, 1, 2, -3, 4)
ROW_WEIGHT = (1.0, 2.0, 2.0, 2.0, 1.0)
RELAY = (4, 6, 7)
ROUND = 12582912.0
STEP = 128

ROOT2 = 2.0**0.5
SIN = [ROOT2 * v for v in (3.141592580044453, -5.167706878911761, 2.5500313770692338,
                           -0.5980451729935192, 0.07722012694435497)]
COS = [-ROOT2 * v for v in (0.9999999534664096, -4.93479285864205, 4.058411913501759,
                            -1.331880156986464, 0.2196967900729894)]


def prep_kernel(spectra, travel, payload):
    for f in range(F):
        re = spectra[f, 0]
        im = spectra[f, 1]
        magnitude = jnp.sqrt(re * re + im * im + 0.5)
        for c, part in enumerate((re, im)):
            value = (part / magnitude).astype(jnp.bfloat16).astype(jnp.float32) * 32768.0
            value = jnp.clip((value + ROUND) - ROUND, -32767.0, 32767.0)
            at = NPT + 32 * f + 16 * c
            payload[at:at + 16, :] = value.astype(jnp.int32).astype(jnp.int16)
    payload[0:NPT, :] = travel[...].T.astype(jnp.int16)


def steer_kernel(bins, *refs):
    payloads, out = refs[:-1], refs[-1]
    rows = 64
    for n, ref in enumerate(payloads):
        def chunk(i, carry, n=n, ref=ref):
            at = pl.ds(pl.multiple_of(i * rows, rows), rows)
            samples = (ref[at, :].astype(jnp.int32) & (NFFT - 1)).astype(jnp.float32)
            for f in range(F):
                scale = bins[f].astype(jnp.float32) * (1.0 / NFFT)
                turns = samples * scale
                r = turns - ((turns + ROUND) - ROUND)
                z = r * r
                s = SIN[4]
                c = COS[4]
                for k in (3, 2, 1, 0):
                    s = s * z + SIN[k]
                    c = c * z + COS[k]
                s = s * r
                out[f, 0, n, at, :] = (1.0 - s * s).astype(jnp.bfloat16)
                out[f, 1, n, at, :] = (s * c).astype(jnp.bfloat16)
            return carry

        lax.fori_loop(0, STEP // rows, chunk, 0)


def steer(bins, payloads):
    n = len(payloads)
    return pl.pallas_call(
        steer_kernel,
        grid=(NPT // STEP,),
        out_shape=jax.ShapeDtypeStruct((F, 2, n, NPT, NST), jnp.bfloat16),
        in_specs=[pl.BlockSpec(memory_space=pltpu.SMEM)]
        + [pl.BlockSpec((STEP, NST), lambda i: (i, 0))] * n,
        out_specs=pl.BlockSpec((F, 2, n, STEP, NST), lambda i: (0, 0, 0, i, 0)),
    )(bins, *payloads)


def decode(sources, block):
    return [
        (a[block].astype(jnp.int32).astype(jnp.float32) * (1.0 / 32768.0)).astype(jnp.bfloat16)
        for a in sources
    ]


def beam_kernel(own_steer, col_steer, row_steer, a0, a1, a2, a3, beam, cols, weights):
    sources = (a0, a1, a2, a3)
    for d in range(4):
        cols[d * NST:(d + 1) * NST, :] = jnp.concatenate(decode(sources, d), axis=0).T

    def coherent(k):
        parts = decode(sources, 0 if k == 0 else 3 + k)
        x = jnp.concatenate(parts, axis=0)
        z = jnp.concatenate([q for v in parts for q in (v[16:32], -v[0:16])], axis=0)
        right = jnp.concatenate([x, z], axis=1)
        for j in range(4):
            at = slice(j * NST, (j + 1) * NST)
            cross = jnp.dot(cols[at, :], right, preferred_element_type=jnp.float32)
            re = cross[:, :NST]
            im = cross[:, NST:]
            inverse = lax.rsqrt(re * re + im * im + 64.0)
            if ROW_WEIGHT[k] != 1.0:
                inverse = inverse * ROW_WEIGHT[k]
            re = (re * inverse).astype(jnp.bfloat16)
            im = (im * inverse).astype(jnp.bfloat16)
            weights[k, at, :NST] = re
            weights[k, at, NST:] = im
            at = slice((4 + j) * NST, (5 + j) * NST)
            weights[k, at, :NST] = -im
            weights[k, at, NST:] = re

    steer_cols = jnp.concatenate(
        [ref for part in range(2) for ref in (own_steer[0, part, 0], *(row_steer[0, part, n] for n in range(3)))],
        axis=1,
    )
    total = None
    coherent(0)
    for k in range(5):
        if k < 4:
            coherent(k + 1)
        image = jnp.dot(steer_cols, weights[k], preferred_element_type=jnp.float32)
        re, im = (own_steer[0, 0, 0], own_steer[0, 1, 0]) if k == 0 else (col_steer[0, 0, k - 1], col_steer[0, 1, k - 1])
        power = re.astype(jnp.float32) * image[:, :NST] + im.astype(jnp.float32) * image[:, NST:]
        total = power if total is None else total + power
    for j in range(4):
        value = jnp.sum(total[j * NST:(j + 1) * NST, :].T, axis=0, keepdims=True) * (1.0 / S)
        beam[0, :, j, :] = jnp.broadcast_to(value, (32, NST))


def beams(own_steer, col_steer, row_steer, spectra):
    piece = pl.BlockSpec((8, 32, NST), lambda f: (0, f, 0))
    phases = lambda n: pl.BlockSpec((1, 2, n, NPT, NST), lambda f: (f, 0, 0, 0, 0))
    return pl.pallas_call(
        beam_kernel,
        grid=(F,),
        out_shape=jax.ShapeDtypeStruct((F, 32, 4, NST), jnp.float32),
        in_specs=[phases(1), phases(4), phases(3), piece, piece, piece, piece],
        out_specs=pl.BlockSpec((1, 32, 4, NST), lambda f: (f, 0, 0, 0)),
        scratch_shapes=[
            pltpu.VMEM((4 * NST, NST), jnp.bfloat16),
            pltpu.VMEM((5, 8 * NST, 2 * NST), jnp.bfloat16),
        ],
        name="beams",
    )(own_steer, col_steer, row_steer, *spectra)


def pack_kernel(place, a0, a1, a2, a3, rows):
    for s, a in enumerate((a0, a1, a2, a3)):
        for n, block in enumerate(RELAY):
            rows[s, n] = a[block]


def pack(place, spectra):
    own = pl.BlockSpec((8, 32, NST), lambda n, place: (0, place[0], 0))
    return pl.pallas_call(
        pack_kernel,
        grid_spec=pltpu.PrefetchScalarGridSpec(
            num_scalar_prefetch=1,
            grid=(1,),
            in_specs=[own] * 4,
            out_specs=pl.BlockSpec((4, 3, 32, NST), lambda n, place: (0, 0, 0, 0)),
        ),
        out_shape=jax.ShapeDtypeStruct((4, 3, 32, NST), jnp.int16),
        name="pack",
    )(place, *spectra)


def tile_kernel(place, rows, a0, a1, a2, a3, coherence, cols, scratch):
    n = pl.program_id(0)
    sources = (a0, a1, a2, a3)

    @pl.when(n == 0)
    def _():
        for d in range(4):
            parts = decode(sources, d)
            x = jnp.concatenate(parts, axis=0)
            y = jnp.concatenate([q for v in parts for q in (-v[16:32], v[0:16])], axis=0)
            cols[d] = jnp.concatenate([x, y], axis=1)

    def emit(parts):
        left = jnp.concatenate(parts, axis=0).T
        for d in range(4):
            cross = jnp.dot(left, cols[d], preferred_element_type=jnp.float32)
            re = cross[:, :NST]
            im = cross[:, NST:]
            inverse = lax.rsqrt(re * re + im * im + 64.0)
            at = pl.ds((place[1] + d) & 3, NST, stride=4)
            scratch[0, at, :] = re * inverse
            scratch[1, at, :] = im * inverse
        coherence[0] = scratch[0].astype(jnp.bfloat16)
        coherence[1] = scratch[1].astype(jnp.bfloat16)

    @pl.when(n < 5)
    def _():
        emit(decode(sources, jnp.where(n == 0, 0, n + 3)))

    @pl.when(n >= 5)
    def _():
        emit(decode([rows.at[k] for k in range(4)], n - 5))


def tile(place, rows, spectra):
    own = pl.BlockSpec((8, 32, NST), lambda n, place: (0, place[0], 0))

    def at(n, place):
        far = jnp.where(n == 3, -3, jnp.where(n < 5, n, jnp.where(n == 5, 3, 5 - n)))
        return (0, (place[2] + far) & 7, 0)

    return pl.pallas_call(
        tile_kernel,
        grid_spec=pltpu.PrefetchScalarGridSpec(
            num_scalar_prefetch=1,
            grid=(8,),
            in_specs=[pl.BlockSpec((4, 3, 32, NST), lambda n, place: (0, 0, 0, 0)), own, own, own, own],
            out_specs=pl.BlockSpec((2, 4 * NST, NST), at),
            scratch_shapes=[
                pltpu.VMEM((4, NST, 2 * NST), jnp.bfloat16),
                pltpu.VMEM((2, 4 * NST, NST), jnp.float32),
            ],
        ),
        out_shape=jax.ShapeDtypeStruct((2, 4 * 1024, NST), jnp.bfloat16),
        name="tile",
    )(place, rows, *spectra)


def from_offset(value, axis, offset):
    size = lax.axis_size(axis)
    return lax.ppermute(value, axis, [((i + offset) % size, i) for i in range(size)])


def from_partner(value, bit):
    return lax.ppermute(value, "win", [(i ^ bit, i) for i in range(4)])


def local(spectra, bins, travel):
    payload = pl.pallas_call(
        prep_kernel,
        out_shape=jax.ShapeDtypeStruct((NPT + 32 * F, NST), jnp.int16),
        name="prep",
    )(spectra, travel)
    place = jnp.stack([lax.axis_index(a) for a in ALL]).astype(jnp.int32)
    by_row = [from_offset(payload, "srow", d) for d in (1, 2, 3)]
    by_col = [from_offset(payload, "scol", d) for d in ROW_OFF[1:]]
    steer0 = steer(bins, [payload])
    steer2 = steer(bins, by_row)
    by_col, steer0, steer2 = lax.optimization_barrier((by_col, steer0, steer2))
    a0 = jnp.stack([v[NPT:] for v in [payload] + by_row + by_col])
    a1 = from_partner(a0, 2)
    a2 = from_partner(a0, 1)
    steer1 = steer(bins, by_col)
    a1, steer1 = lax.optimization_barrier((a1, steer1))
    a3 = from_partner(a1, 1)
    sources = (a0, a1, a2, a3)
    packed = pack(place, sources)
    rows = from_offset(packed, "scol", 2)
    partial = beams(steer0, steer1, steer2, sources)
    shares = lax.all_to_all(partial.reshape(128, 4, NST), ALL, 0, 0, tiled=True)
    coherence = tile(place, rows, sources)
    beam = shares.reshape(4, 32, 4, NST).sum(axis=1).reshape(1, 4 * NPT)
    return coherence.reshape(1, 2, 1024, 4, NST), beam


def solution(mesh):
    placed = (P(None, None, "win", ("srow", "scol")), P(), P(("srow", "scol"), "win"))
    return jax.shard_map(
        local,
        mesh=mesh,
        in_specs=placed,
        out_specs=(P("win", None, "srow", None, "scol"), P("win", None)),
        check_vma=False,
    )
```

```python
import jax
import jax.numpy as jnp
from jax import lax
from jax.experimental import pallas as pl
from jax.experimental.pallas import tpu as pltpu
from jax.sharding import PartitionSpec as P


S = 4096
NFFT = 4096
F = 4
NST = 128
NPT = 512
ALL = ("win", "srow", "scol")
ROW_OFF = (0, 1, 2, -3, 4)
ROW_WEIGHT = (1.0, 2.0, 2.0, 2.0, 1.0)
RELAY = (4, 6, 7)
ROUND = 12582912.0

ROOT2 = 2.0**0.5
SIN = [ROOT2 * v for v in (3.141592580044453, -5.167706878911761, 2.5500313770692338,
                           -0.5980451729935192, 0.07722012694435497)]
COS = [-ROOT2 * v for v in (0.9999999534664096, -4.93479285864205, 4.058411913501759,
                            -1.331880156986464, 0.2196967900729894)]


def prep_kernel(spectra, travel, payload):
    for f in range(F):
        re = spectra[f, 0]
        im = spectra[f, 1]
        magnitude = jnp.sqrt(re * re + im * im + 0.5)
        for c, part in enumerate((re, im)):
            value = (part / magnitude).astype(jnp.bfloat16).astype(jnp.float32) * 32768.0
            value = jnp.clip((value + ROUND) - ROUND, -32767.0, 32767.0)
            at = NPT + 32 * f + 16 * c
            payload[at:at + 16, :] = value.astype(jnp.int32).astype(jnp.int16)
    payload[0:NPT, :] = travel[...].T.astype(jnp.int16)


def on_chip(*arrays):
    return [pltpu.with_memory_space_constraint(v, pltpu.VMEM) for v in arrays]


def vmem(n):
    return [pl.BlockSpec(memory_space=pltpu.VMEM)] * n


SMEM = pl.BlockSpec(memory_space=pltpu.SMEM)
LIMIT = pltpu.CompilerParams(vmem_limit_bytes=16 * 2**20)


def steer_kernel(bins, *refs):
    payloads, out = refs[:-1], refs[-1]
    rows = 64
    for n, ref in enumerate(payloads):
        def chunk(i, carry, n=n, ref=ref):
            at = pl.ds(pl.multiple_of(i * rows, rows), rows)
            samples = (ref[at, :].astype(jnp.int32) & (NFFT - 1)).astype(jnp.float32)
            for f in range(F):
                scale = bins[f].astype(jnp.float32) * (1.0 / NFFT)
                turns = samples * scale
                r = turns - ((turns + ROUND) - ROUND)
                z = r * r
                s = SIN[4]
                c = COS[4]
                for k in (3, 2, 1, 0):
                    s = s * z + SIN[k]
                    c = c * z + COS[k]
                s = s * r
                out[f, 0, n, at, :] = (1.0 - s * s).astype(jnp.bfloat16)
                out[f, 1, n, at, :] = (s * c).astype(jnp.bfloat16)
            return carry

        lax.fori_loop(0, NPT // rows, chunk, 0)


def steer(bins, payloads):
    n = len(payloads)
    return pl.pallas_call(
        steer_kernel,
        out_shape=pltpu.VMEM((F, 2, n, NPT, NST), jnp.bfloat16),
        in_specs=[SMEM] + vmem(n),
        out_specs=vmem(1)[0],
        compiler_params=LIMIT,
    )(bins, *on_chip(*payloads))


def stack_kernel(*refs):
    for n, ref in enumerate(refs[:-1]):
        refs[-1][n] = ref[NPT:NPT + 32 * F, :]


def stack(payloads):
    return pl.pallas_call(
        stack_kernel,
        out_shape=pltpu.VMEM((len(payloads), 32 * F, NST), jnp.int16),
        in_specs=vmem(len(payloads)),
        out_specs=vmem(1)[0],
        compiler_params=LIMIT,
        name="stack",
    )(*on_chip(*payloads))


def decode(sources, block, f):
    at = pl.ds(pl.multiple_of(32 * f, 32), 32)
    return [
        (a[block, at, :].astype(jnp.int32).astype(jnp.float32) * (1.0 / 32768.0)).astype(jnp.bfloat16)
        for a in sources
    ]


def beam_kernel(own_steer, col_steer, row_steer, a0, a1, a2, a3, beam, cols, weights):
    sources = (a0, a1, a2, a3)

    def one(f, carry):
        for d in range(4):
            cols[d * NST:(d + 1) * NST, :] = jnp.concatenate(decode(sources, d, f), axis=0).T

        def coherent(k):
            parts = decode(sources, 0 if k == 0 else 3 + k, f)
            x = jnp.concatenate(parts, axis=0)
            z = jnp.concatenate([q for v in parts for q in (v[16:32], -v[0:16])], axis=0)
            right = jnp.concatenate([x, z], axis=1)
            for j in range(4):
                at = slice(j * NST, (j + 1) * NST)
                cross = jnp.dot(cols[at, :], right, preferred_element_type=jnp.float32)
                re = cross[:, :NST]
                im = cross[:, NST:]
                inverse = lax.rsqrt(re * re + im * im + 64.0)
                if ROW_WEIGHT[k] != 1.0:
                    inverse = inverse * ROW_WEIGHT[k]
                re = (re * inverse).astype(jnp.bfloat16)
                im = (im * inverse).astype(jnp.bfloat16)
                weights[k, at, :NST] = re
                weights[k, at, NST:] = im
                at = slice((4 + j) * NST, (5 + j) * NST)
                weights[k, at, :NST] = -im
                weights[k, at, NST:] = re

        steer_cols = jnp.concatenate(
            [ref for part in range(2) for ref in (own_steer[f, part, 0], *(row_steer[f, part, n] for n in range(3)))],
            axis=1,
        )
        total = None
        coherent(0)
        for k in range(5):
            if k < 4:
                coherent(k + 1)
            image = jnp.dot(steer_cols, weights[k], preferred_element_type=jnp.float32)
            re, im = (own_steer[f, 0, 0], own_steer[f, 1, 0]) if k == 0 else (col_steer[f, 0, k - 1], col_steer[f, 1, k - 1])
            power = re.astype(jnp.float32) * image[:, :NST] + im.astype(jnp.float32) * image[:, NST:]
            total = power if total is None else total + power
        for j in range(4):
            value = jnp.sum(total[j * NST:(j + 1) * NST, :].T, axis=0, keepdims=True) * (1.0 / S)
            beam[f, :, j, :] = jnp.broadcast_to(value, (32, NST))
        return carry

    lax.fori_loop(0, F, one, 0)


def beams(own_steer, col_steer, row_steer, spectra):
    return pl.pallas_call(
        beam_kernel,
        out_shape=pltpu.VMEM((F, 32, 4, NST), jnp.float32),
        in_specs=vmem(7),
        out_specs=vmem(1)[0],
        scratch_shapes=[
            pltpu.VMEM((4 * NST, NST), jnp.bfloat16),
            pltpu.VMEM((5, 8 * NST, 2 * NST), jnp.bfloat16),
        ],
        compiler_params=LIMIT,
        name="beams",
    )(*on_chip(own_steer, col_steer, row_steer, *spectra))


def pack_kernel(place, a0, a1, a2, a3, rows):
    at = pl.ds(pl.multiple_of(32 * place[0], 32), 32)
    for s, a in enumerate((a0, a1, a2, a3)):
        for n, block in enumerate(RELAY):
            rows[s, n] = a[block, at, :]


def pack(place, spectra):
    return pl.pallas_call(
        pack_kernel,
        out_shape=pltpu.VMEM((4, 3, 32, NST), jnp.int16),
        in_specs=[SMEM] + vmem(4),
        out_specs=vmem(1)[0],
        compiler_params=LIMIT,
        name="pack",
    )(place, *on_chip(*spectra))


def tile_kernel(place, rows, a0, a1, a2, a3, coherence, cols, scratch):
    n = pl.program_id(0)
    sources = (a0, a1, a2, a3)

    @pl.when(n == 0)
    def _():
        for d in range(4):
            parts = decode(sources, d, place[0])
            x = jnp.concatenate(parts, axis=0)
            y = jnp.concatenate([q for v in parts for q in (-v[16:32], v[0:16])], axis=0)
            cols[d] = jnp.concatenate([x, y], axis=1)

    def emit(parts):
        left = jnp.concatenate(parts, axis=0).T
        for d in range(4):
            cross = jnp.dot(left, cols[d], preferred_element_type=jnp.float32)
            re = cross[:, :NST]
            im = cross[:, NST:]
            inverse = lax.rsqrt(re * re + im * im + 64.0)
            at = pl.ds((place[1] + d) & 3, NST, stride=4)
            scratch[0, at, :] = re * inverse
            scratch[1, at, :] = im * inverse
        coherence[0] = scratch[0].astype(jnp.bfloat16)
        coherence[1] = scratch[1].astype(jnp.bfloat16)

    @pl.when(n < 5)
    def _():
        emit(decode(sources, jnp.where(n == 0, 0, n + 3), place[0]))

    @pl.when(n >= 5)
    def _():
        emit(decode([rows.at[k] for k in range(4)], n - 5, 0))


def tile(place, rows, spectra):
    def at(n, place):
        far = jnp.where(n == 3, -3, jnp.where(n < 5, n, jnp.where(n == 5, 3, 5 - n)))
        return (0, (place[2] + far) & 7, 0)

    return pl.pallas_call(
        tile_kernel,
        grid_spec=pltpu.PrefetchScalarGridSpec(
            num_scalar_prefetch=1,
            grid=(8,),
            in_specs=vmem(5),
            out_specs=pl.BlockSpec((2, 4 * NST, NST), at),
            scratch_shapes=[
                pltpu.VMEM((4, NST, 2 * NST), jnp.bfloat16),
                pltpu.VMEM((2, 4 * NST, NST), jnp.float32),
            ],
        ),
        out_shape=jax.ShapeDtypeStruct((2, 4 * 1024, NST), jnp.bfloat16),
        compiler_params=LIMIT,
        name="tile",
    )(place, *on_chip(rows, *spectra))


def from_offset(value, axis, offset):
    size = lax.axis_size(axis)
    return lax.ppermute(value, axis, [((i + offset) % size, i) for i in range(size)])


def from_partner(value, bit):
    return lax.ppermute(value, "win", [(i ^ bit, i) for i in range(4)])


def local(spectra, bins, travel):
    payload = pl.pallas_call(
        prep_kernel,
        out_shape=pltpu.VMEM((NPT + 32 * F, NST), jnp.int16),
        compiler_params=LIMIT,
        name="prep",
    )(spectra, travel)
    place = jnp.stack([lax.axis_index(a) for a in ALL]).astype(jnp.int32)
    by_row = [from_offset(payload, "srow", d) for d in (1, 2, 3)]
    by_col = [from_offset(payload, "scol", d) for d in ROW_OFF[1:]]
    steer0 = steer(bins, [payload])
    steer2 = steer(bins, by_row)
    by_col, steer0, steer2 = lax.optimization_barrier((by_col, steer0, steer2))
    a0 = stack([payload] + by_row + by_col)
    a1 = from_partner(a0, 2)
    a2 = from_partner(a0, 1)
    steer1 = steer(bins, by_col)
    a1, steer1 = lax.optimization_barrier((a1, steer1))
    a3 = from_partner(a1, 1)
    sources = (a0, a1, a2, a3)
    packed = pack(place, sources)
    rows = from_offset(packed, "scol", 2)
    partial = beams(steer0, steer1, steer2, sources)
    shares = lax.all_to_all(partial.reshape(128, 4, NST), ALL, 0, 0, tiled=True)
    coherence = tile(place, rows, sources)
    beam = shares.reshape(4, 32, 4, NST).sum(axis=1).reshape(1, 4 * NPT)
    return coherence.reshape(1, 2, 1024, 4, NST), beam


def solution(mesh):
    placed = (P(None, None, "win", ("srow", "scol")), P(), P(("srow", "scol"), "win"))
    return jax.shard_map(
        local,
        mesh=mesh,
        in_specs=placed,
        out_specs=(P("win", None, "srow", None, "scol"), P("win", None)),
        check_vma=False,
    )
```

```python
import jax
import jax.numpy as jnp
from jax import lax
from jax.experimental import pallas as pl
from jax.experimental.pallas import tpu as pltpu
from jax.sharding import PartitionSpec as P


S = 4096
NFFT = 4096
F = 4
NST = 128
NPT = 512
ALL = ("win", "srow", "scol")
ROW_OFF = (0, 1, 2, -3, 4)
WEIGHT = ((1, 2, 1), (2, 2, 2, 2), (2, 2, 2, 2), (2, 2, 2, 2), (1, 2, 1))
RELAY = (4, 6, 7)
ROUND = 12582912.0

ROOT2 = 2.0**0.5
SIN = [ROOT2 * v for v in (3.141592580044453, -5.167706878911761, 2.5500313770692338,
                           -0.5980451729935192, 0.07722012694435497)]
COS = [-ROOT2 * v for v in (0.9999999534664096, -4.93479285864205, 4.058411913501759,
                            -1.331880156986464, 0.2196967900729894)]


def prep_kernel(spectra, travel, payload):
    for f in range(F):
        re = spectra[f, 0]
        im = spectra[f, 1]
        magnitude = jnp.sqrt(re * re + im * im + 0.5)
        for c, part in enumerate((re, im)):
            value = (part / magnitude).astype(jnp.bfloat16).astype(jnp.float32) * 32768.0
            value = jnp.clip((value + ROUND) - ROUND, -32767.0, 32767.0)
            at = NPT + 32 * f + 16 * c
            payload[at:at + 16, :] = value.astype(jnp.int32).astype(jnp.int16)
    payload[0:NPT, :] = travel[...].T.astype(jnp.int16)


def on_chip(*arrays):
    return [pltpu.with_memory_space_constraint(v, pltpu.VMEM) for v in arrays]


def vmem(n):
    return [pl.BlockSpec(memory_space=pltpu.VMEM)] * n


SMEM = pl.BlockSpec(memory_space=pltpu.SMEM)
LIMIT = pltpu.CompilerParams(vmem_limit_bytes=16 * 2**20)


def steer_kernel(bins, *refs):
    payloads, out = refs[:-1], refs[-1]
    rows = 64
    for n, ref in enumerate(payloads):
        def chunk(i, carry, n=n, ref=ref):
            at = pl.ds(pl.multiple_of(i * rows, rows), rows)
            samples = (ref[at, :].astype(jnp.int32) & (NFFT - 1)).astype(jnp.float32)
            for f in range(F):
                scale = bins[f].astype(jnp.float32) * (1.0 / NFFT)
                turns = samples * scale
                r = turns - ((turns + ROUND) - ROUND)
                z = r * r
                s = SIN[4]
                c = COS[4]
                for k in (3, 2, 1, 0):
                    s = s * z + SIN[k]
                    c = c * z + COS[k]
                s = s * r
                out[f, 0, n, at, :] = (1.0 - s * s).astype(jnp.bfloat16)
                out[f, 1, n, at, :] = (s * c).astype(jnp.bfloat16)
            return carry

        lax.fori_loop(0, NPT // rows, chunk, 0)


def steer(bins, payloads):
    n = len(payloads)
    return pl.pallas_call(
        steer_kernel,
        out_shape=pltpu.VMEM((F, 2, n, NPT, NST), jnp.bfloat16),
        in_specs=[SMEM] + vmem(n),
        out_specs=vmem(1)[0],
        compiler_params=LIMIT,
    )(pltpu.with_memory_space_constraint(bins, pltpu.SMEM), *on_chip(*payloads))


def stack_kernel(*refs):
    for n, ref in enumerate(refs[:-1]):
        refs[-1][n] = ref[NPT:NPT + 32 * F, :]


def stack(payloads):
    return pl.pallas_call(
        stack_kernel,
        out_shape=pltpu.VMEM((len(payloads), 32 * F, NST), jnp.int16),
        in_specs=vmem(len(payloads)),
        out_specs=vmem(1)[0],
        compiler_params=LIMIT,
        name="stack",
    )(*on_chip(*payloads))


def decode(sources, block, f):
    at = pl.ds(pl.multiple_of(32 * f, 32), 32)
    return [
        (a[block, at, :].astype(jnp.int32).astype(jnp.float32) * (1.0 / 32768.0)).astype(jnp.bfloat16)
        for a in sources
    ]


def beam_kernel(own_steer, col_steer, row_steer, a0, a1, a2, a3, beam, cols, weights):
    sources = (a0, a1, a2, a3)

    def one(f, carry):
        for d in range(4):
            cols[d * NST:(d + 1) * NST, :] = jnp.concatenate(decode(sources, d, f), axis=0).T

        def coherent(k):
            parts = decode(sources, 0 if k == 0 else 3 + k, f)
            x = jnp.concatenate(parts, axis=0)
            z = jnp.concatenate([q for v in parts for q in (v[16:32], -v[0:16])], axis=0)
            right = jnp.concatenate([x, z], axis=1)
            for j, weight in enumerate(WEIGHT[k]):
                at = slice(j * NST, (j + 1) * NST)
                cross = jnp.dot(cols[at, :], right, preferred_element_type=jnp.float32)
                re = cross[:, :NST]
                im = cross[:, NST:]
                inverse = lax.rsqrt(re * re + im * im + 64.0)
                if weight == 2:
                    inverse = inverse + inverse
                re = (re * inverse).astype(jnp.bfloat16)
                im = (im * inverse).astype(jnp.bfloat16)
                at = slice(2 * j * NST, (2 * j + 1) * NST)
                weights[k, at, :NST] = re
                weights[k, at, NST:] = im
                at = slice((2 * j + 1) * NST, (2 * j + 2) * NST)
                weights[k, at, :NST] = -im
                weights[k, at, NST:] = re

        steer_cols = jnp.concatenate(
            [own_steer[f, 0, 0], own_steer[f, 1, 0]] + [row_steer[f, part, n] for n in range(3) for part in range(2)],
            axis=1,
        )
        total = None
        coherent(0)
        for k in range(5):
            if k < 4:
                coherent(k + 1)
            depth = 2 * NST * len(WEIGHT[k])
            image = jnp.dot(steer_cols[:, :depth], weights[k, :depth], preferred_element_type=jnp.float32)
            re, im = (own_steer[f, 0, 0], own_steer[f, 1, 0]) if k == 0 else (col_steer[f, 0, k - 1], col_steer[f, 1, k - 1])
            power = re.astype(jnp.float32) * image[:, :NST] + im.astype(jnp.float32) * image[:, NST:]
            total = power if total is None else total + power
        for j in range(4):
            value = jnp.sum(total[j * NST:(j + 1) * NST, :].T, axis=0, keepdims=True) * (1.0 / S)
            beam[f, :, j, :] = jnp.broadcast_to(value, (32, NST))
        return carry

    lax.fori_loop(0, F, one, 0)


def beams(own_steer, col_steer, row_steer, spectra):
    return pl.pallas_call(
        beam_kernel,
        out_shape=pltpu.VMEM((F, 32, 4, NST), jnp.float32),
        in_specs=vmem(7),
        out_specs=vmem(1)[0],
        scratch_shapes=[
            pltpu.VMEM((4 * NST, NST), jnp.bfloat16),
            pltpu.VMEM((5, 8 * NST, 2 * NST), jnp.bfloat16),
        ],
        compiler_params=LIMIT,
        name="beams",
    )(*on_chip(own_steer, col_steer, row_steer, *spectra))


def pack_kernel(a0, a1, a2, a3, rows):
    at = pl.ds(pl.multiple_of(32 * lax.axis_index("win"), 32), 32)
    for s, a in enumerate((a0, a1, a2, a3)):
        for n, block in enumerate(RELAY):
            rows[s, n] = a[block, at, :]


def pack(spectra):
    return pl.pallas_call(
        pack_kernel,
        out_shape=pltpu.VMEM((4, 3, 32, NST), jnp.int16),
        in_specs=vmem(4),
        out_specs=vmem(1)[0],
        compiler_params=LIMIT,
        name="pack",
    )(*on_chip(*spectra))


def tile_kernel(rows, a0, a1, a2, a3, coherence, cols, scratch, ready, sems):
    w, r, c = (lax.axis_index(a) for a in ALL)
    sources = (a0, a1, a2, a3)
    for d in range(4):
        parts = decode(sources, d, w)
        x = jnp.concatenate(parts, axis=0)
        y = jnp.concatenate([q for v in parts for q in (-v[16:32], v[0:16])], axis=0)
        cols[d] = jnp.concatenate([x, y], axis=1)

    def send(offset, slot):
        at = pl.ds(pl.multiple_of(((c + offset) & 7) * (4 * NST), 4 * NST), 4 * NST)
        return pltpu.make_async_copy(ready.at[slot], coherence.at[:, at, :], sems.at[slot])

    def emit(parts, slot):
        left = jnp.concatenate(parts, axis=0).T
        for d in range(4):
            cross = jnp.dot(left, cols[d], preferred_element_type=jnp.float32)
            re = cross[:, :NST]
            im = cross[:, NST:]
            inverse = lax.rsqrt(re * re + im * im + 64.0)
            at = pl.ds((r + d) & 3, NST, stride=4)
            scratch[0, at, :] = re * inverse
            scratch[1, at, :] = im * inverse
        ready[slot, 0] = scratch[0].astype(jnp.bfloat16)
        ready[slot, 1] = scratch[1].astype(jnp.bfloat16)

    for n, offset in enumerate(ROW_OFF):
        emit(decode(sources, 0 if n == 0 else 3 + n, w), n)
        send(offset, n).start()
    for n, offset in enumerate((3, -1, -2)):
        emit(decode([rows.at[k] for k in range(4)], n, 0), 5 + n)
        send(offset, 5 + n).start()
    for n, offset in enumerate(ROW_OFF + (3, -1, -2)):
        send(offset, n).wait()


def tile(rows, spectra):
    return pl.pallas_call(
        tile_kernel,
        in_specs=vmem(5),
        out_specs=pl.BlockSpec(memory_space=pl.ANY),
        scratch_shapes=[
            pltpu.VMEM((4, NST, 2 * NST), jnp.bfloat16),
            pltpu.VMEM((2, 4 * NST, NST), jnp.float32),
            pltpu.VMEM((8, 2, 4 * NST, NST), jnp.bfloat16),
            pltpu.SemaphoreType.DMA((8,)),
        ],
        out_shape=jax.ShapeDtypeStruct((2, 4 * 1024, NST), jnp.bfloat16),
        compiler_params=LIMIT,
        name="tile",
    )(*on_chip(rows, *spectra))


def from_offset(value, axis, offset):
    size = lax.axis_size(axis)
    return lax.ppermute(value, axis, [((i + offset) % size, i) for i in range(size)])


def from_partner(value, bit):
    return lax.ppermute(value, "win", [(i ^ bit, i) for i in range(4)])


def local(spectra, bins, travel):
    payload = pl.pallas_call(
        prep_kernel,
        out_shape=pltpu.VMEM((NPT + 32 * F, NST), jnp.int16),
        compiler_params=LIMIT,
        name="prep",
    )(spectra, travel)
    by_row = [from_offset(payload, "srow", d) for d in (1, 2, 3)]
    by_col = [from_offset(payload, "scol", d) for d in ROW_OFF[1:]]
    steer0 = steer(bins, [payload])
    steer2 = steer(bins, by_row)
    by_col, steer0, steer2 = lax.optimization_barrier((by_col, steer0, steer2))
    a0 = stack([payload] + by_row + by_col)
    a1 = from_partner(a0, 2)
    a2 = from_partner(a0, 1)
    steer1 = steer(bins, by_col)
    a1, steer1 = lax.optimization_barrier((a1, steer1))
    a3 = from_partner(a1, 1)
    sources = (a0, a1, a2, a3)
    packed = pack(sources)
    rows = from_offset(packed, "scol", 2)
    partial = beams(steer0, steer1, steer2, sources)
    shares = lax.all_to_all(partial.reshape(128, 4, NST), ALL, 0, 0, tiled=True)
    coherence = tile(rows, sources)
    beam = shares.reshape(4, 32, 4, NST).sum(axis=1).reshape(1, 4 * NPT)
    return coherence.reshape(1, 2, 1024, 4, NST), beam


def solution(mesh):
    placed = (P(None, None, "win", ("srow", "scol")), P(), P(("srow", "scol"), "win"))
    return jax.shard_map(
        local,
        mesh=mesh,
        in_specs=placed,
        out_specs=(P("win", None, "srow", None, "scol"), P("win", None)),
        check_vma=False,
    )
```

```python
import jax
import jax.numpy as jnp
from jax import lax
from jax.experimental import pallas as pl
from jax.experimental.pallas import tpu as pltpu
from jax.sharding import PartitionSpec as P

S = 4096
NFFT = 4096
F = 4
NST = 128
NPT = 512
ALL = ("win", "srow", "scol")
ROW_OFF = (0, 1, 2, -3, 4)
WEIGHT = ((1, 2, 1), (2, 2, 2, 2), (2, 2, 2, 2), (2, 2, 2, 2), (1, 2, 1))
RELAY = (4, 6, 7)
ROUND = 12582912.0

ROOT2 = 2.0**0.5
SIN = [ROOT2 * v for v in (3.141592580044453, -5.167706878911761, 2.5500313770692338,
                           -0.5980451729935192, 0.07722012694435497)]
COS = [-ROOT2 * v for v in (0.9999999534664096, -4.93479285864205, 4.058411913501759,
                            -1.331880156986464, 0.2196967900729894)]


def prep_kernel(spectra_hbm, travel_hbm, payload, spectra, travel, sems):
    moves = [
        pltpu.make_async_copy(spectra_hbm, spectra, sems.at[0]),
        pltpu.make_async_copy(travel_hbm, travel, sems.at[1]),
    ]
    for move in moves:
        move.start()
    moves[0].wait()
    for f in range(F):
        re = spectra[f, 0]
        im = spectra[f, 1]
        magnitude = jnp.sqrt(re * re + im * im + 0.5)
        for c, part in enumerate((re, im)):
            value = (part / magnitude).astype(jnp.bfloat16).astype(jnp.float32) * 32768.0
            value = jnp.clip((value + ROUND) - ROUND, -32767.0, 32767.0)
            at = NPT + 32 * f + 16 * c
            payload[at:at + 16, :] = value.astype(jnp.int32).astype(jnp.int16)
    moves[1].wait()
    payload[0:NPT, :] = travel[...].T.astype(jnp.int16)


def on_chip(*arrays):
    return [pltpu.with_memory_space_constraint(v, pltpu.VMEM) for v in arrays]


def vmem(n):
    return [pl.BlockSpec(memory_space=pltpu.VMEM)] * n


SMEM = pl.BlockSpec(memory_space=pltpu.SMEM)
LIMIT = pltpu.CompilerParams(vmem_limit_bytes=16 * 2**20)


def steer_kernel(bins, *refs):
    payloads, out = refs[:-1], refs[-1]
    rows = 64
    for n, ref in enumerate(payloads):
        def chunk(i, carry, n=n, ref=ref):
            at = pl.ds(pl.multiple_of(i * rows, rows), rows)
            samples = (ref[at, :].astype(jnp.int32) & (NFFT - 1)).astype(jnp.float32)
            for f in range(F):
                scale = bins[f].astype(jnp.float32) * (1.0 / NFFT)
                turns = samples * scale
                r = turns - ((turns + ROUND) - ROUND)
                z = r * r
                s = SIN[4]
                c = COS[4]
                for k in (3, 2, 1, 0):
                    s = s * z + SIN[k]
                    c = c * z + COS[k]
                s = s * r
                out[f, 0, n, at, :] = (1.0 - s * s).astype(jnp.bfloat16)
                out[f, 1, n, at, :] = (s * c).astype(jnp.bfloat16)
            return carry

        lax.fori_loop(0, NPT // rows, chunk, 0)


def steer(bins, payloads):
    n = len(payloads)
    return pl.pallas_call(
        steer_kernel,
        out_shape=pltpu.VMEM((F, 2, n, NPT, NST), jnp.bfloat16),
        in_specs=[SMEM] + vmem(n),
        out_specs=vmem(1)[0],
        compiler_params=LIMIT,
    )(pltpu.with_memory_space_constraint(bins, pltpu.SMEM), *on_chip(*payloads))


def stack_kernel(*refs):
    for n, ref in enumerate(refs[:-1]):
        refs[-1][n] = ref[NPT:NPT + 32 * F, :]


def stack(payloads):
    return pl.pallas_call(
        stack_kernel,
        out_shape=pltpu.VMEM((len(payloads), 32 * F, NST), jnp.int16),
        in_specs=vmem(len(payloads)),
        out_specs=vmem(1)[0],
        compiler_params=LIMIT,
        name="stack",
    )(*on_chip(*payloads))


def decode(sources, block, f):
    at = pl.ds(pl.multiple_of(32 * f, 32), 32)
    return [
        (a[block, at, :].astype(jnp.int32).astype(jnp.float32) * (1.0 / 32768.0)).astype(jnp.bfloat16)
        for a in sources
    ]


def beam_kernel(own_steer, col_steer, row_steer, a0, a1, a2, a3, beam, cols, weights):
    sources = (a0, a1, a2, a3)

    def one(f, carry):
        for d in range(4):
            cols[d * NST:(d + 1) * NST, :] = jnp.concatenate(decode(sources, d, f), axis=0).T

        def coherent(k):
            parts = decode(sources, 0 if k == 0 else 3 + k, f)
            x = jnp.concatenate(parts, axis=0)
            z = jnp.concatenate([q for v in parts for q in (v[16:32], -v[0:16])], axis=0)
            right = jnp.concatenate([x, z], axis=1)
            for j, weight in enumerate(WEIGHT[k]):
                at = slice(j * NST, (j + 1) * NST)
                cross = jnp.dot(cols[at, :], right, preferred_element_type=jnp.float32)
                re = cross[:, :NST]
                im = cross[:, NST:]
                inverse = lax.rsqrt(re * re + im * im + 64.0)
                if weight == 2:
                    inverse = inverse + inverse
                re = (re * inverse).astype(jnp.bfloat16)
                im = (im * inverse).astype(jnp.bfloat16)
                at = slice(2 * j * NST, (2 * j + 1) * NST)
                weights[k, at, :NST] = re
                weights[k, at, NST:] = im
                at = slice((2 * j + 1) * NST, (2 * j + 2) * NST)
                weights[k, at, :NST] = -im
                weights[k, at, NST:] = re

        steer_cols = jnp.concatenate(
            [own_steer[f, 0, 0], own_steer[f, 1, 0]] + [row_steer[f, part, n] for n in range(3) for part in range(2)],
            axis=1,
        )
        total = None
        coherent(0)
        for k in range(5):
            if k < 4:
                coherent(k + 1)
            depth = 2 * NST * len(WEIGHT[k])
            image = jnp.dot(steer_cols[:, :depth], weights[k, :depth], preferred_element_type=jnp.float32)
            re, im = (own_steer[f, 0, 0], own_steer[f, 1, 0]) if k == 0 else (col_steer[f, 0, k - 1], col_steer[f, 1, k - 1])
            power = re.astype(jnp.float32) * image[:, :NST] + im.astype(jnp.float32) * image[:, NST:]
            total = power if total is None else total + power
        for j in range(4):
            value = jnp.sum(total[j * NST:(j + 1) * NST, :].T, axis=0, keepdims=True) * (1.0 / S)
            beam[f, :, j, :] = jnp.broadcast_to(value, (32, NST))
        return carry

    lax.fori_loop(0, F, one, 0)


def beams(own_steer, col_steer, row_steer, spectra):
    return pl.pallas_call(
        beam_kernel,
        out_shape=pltpu.VMEM((F, 32, 4, NST), jnp.float32),
        in_specs=vmem(7),
        out_specs=vmem(1)[0],
        scratch_shapes=[
            pltpu.VMEM((4 * NST, NST), jnp.bfloat16),
            pltpu.VMEM((5, 8 * NST, 2 * NST), jnp.bfloat16),
        ],
        compiler_params=LIMIT,
        name="beams",
    )(*on_chip(own_steer, col_steer, row_steer, *spectra))


def pack_kernel(a0, a1, a2, a3, rows):
    at = pl.ds(pl.multiple_of(32 * lax.axis_index("win"), 32), 32)
    for s, a in enumerate((a0, a1, a2, a3)):
        for n, block in enumerate(RELAY):
            rows[s, n] = a[block, at, :]


def pack(spectra):
    return pl.pallas_call(
        pack_kernel,
        out_shape=pltpu.VMEM((4, 3, 32, NST), jnp.int16),
        in_specs=vmem(4),
        out_specs=vmem(1)[0],
        compiler_params=LIMIT,
        name="pack",
    )(*on_chip(*spectra))


def fill_columns(sources, f, cols):
    for d in range(4):
        parts = decode(sources, d, f)
        x = jnp.concatenate(parts, axis=0)
        y = jnp.concatenate([q for v in parts for q in (-v[16:32], v[0:16])], axis=0)
        cols[d] = jnp.concatenate([x, y], axis=1)


def emit(parts, cols, r, scratch, ready):
    left = jnp.concatenate(parts, axis=0).T
    for d in range(4):
        cross = jnp.dot(left, cols[d], preferred_element_type=jnp.float32)
        re = cross[:, :NST]
        im = cross[:, NST:]
        inverse = lax.rsqrt(re * re + im * im + 64.0)
        at = pl.ds((r + d) & 3, NST, stride=4)
        scratch[0, at, :] = re * inverse
        scratch[1, at, :] = im * inverse
    ready[0] = scratch[0].astype(jnp.bfloat16)
    ready[1] = scratch[1].astype(jnp.bfloat16)


def block_copy(ready, coherence, offset, sem):
    row = (lax.axis_index("scol") + offset) & 7
    at = pl.ds(pl.multiple_of(row * (4 * NST), 4 * NST), 4 * NST)
    return pltpu.make_async_copy(ready, coherence.at[:, at, :], sem)


def near_kernel(a0, a1, a2, a3, coherence, cols, scratch, ready, sems):
    w, r = lax.axis_index("win"), lax.axis_index("srow")
    sources = (a0, a1, a2, a3)
    fill_columns(sources, w, cols)
    for n, offset in enumerate(ROW_OFF):
        emit(decode(sources, 0 if n == 0 else 3 + n, w), cols, r, scratch, ready.at[n])
        block_copy(ready.at[n], coherence, offset, sems.at[n]).start()
    for n, offset in enumerate(ROW_OFF):
        block_copy(ready.at[n], coherence, offset, sems.at[n]).wait()


def far_kernel(rows, a0, a1, a2, a3, old, coherence, cols, scratch, ready, sems):
    w, r = lax.axis_index("win"), lax.axis_index("srow")
    fill_columns((a0, a1, a2, a3), w, cols)
    for n, offset in enumerate((3, -1, -2)):
        emit(decode([rows.at[k] for k in range(4)], n, 0), cols, r, scratch, ready.at[n])
        block_copy(ready.at[n], coherence, offset, sems.at[n]).start()
    for n, offset in enumerate((3, -1, -2)):
        block_copy(ready.at[n], coherence, offset, sems.at[n]).wait()


def tile_scratch(n):
    return [
        pltpu.VMEM((4, NST, 2 * NST), jnp.bfloat16),
        pltpu.VMEM((2, 4 * NST, NST), jnp.float32),
        pltpu.VMEM((n, 2, 4 * NST, NST), jnp.bfloat16),
        pltpu.SemaphoreType.DMA((n,)),
    ]


TILE = jax.ShapeDtypeStruct((2, 4 * 1024, NST), jnp.bfloat16)
ANY = pl.BlockSpec(memory_space=pl.ANY)


def near_tile(spectra):
    return pl.pallas_call(
        near_kernel,
        in_specs=vmem(4),
        out_specs=ANY,
        scratch_shapes=tile_scratch(5),
        out_shape=TILE,
        compiler_params=LIMIT,
        name="near",
    )(*on_chip(*spectra))


def far_tile(rows, spectra, coherence):
    return pl.pallas_call(
        far_kernel,
        in_specs=vmem(5) + [ANY],
        out_specs=ANY,
        scratch_shapes=tile_scratch(3),
        out_shape=TILE,
        input_output_aliases={5: 0},
        compiler_params=LIMIT,
        name="far",
    )(*on_chip(rows, *spectra), coherence)


def from_offset(value, axis, offset):
    size = lax.axis_size(axis)
    return lax.ppermute(value, axis, [((i + offset) % size, i) for i in range(size)])


def from_partner(value, bit):
    return lax.ppermute(value, "win", [(i ^ bit, i) for i in range(4)])


def local(spectra, bins, travel):
    payload = pl.pallas_call(
        prep_kernel,
        out_shape=pltpu.VMEM((NPT + 32 * F, NST), jnp.int16),
        in_specs=[pl.BlockSpec(memory_space=pl.ANY)] * 2,
        out_specs=vmem(1)[0],
        scratch_shapes=[
            pltpu.VMEM(spectra.shape, jnp.float32),
            pltpu.VMEM(travel.shape, jnp.int32),
            pltpu.SemaphoreType.DMA((2,)),
        ],
        compiler_params=LIMIT,
        name="prep",
    )(*(pltpu.with_memory_space_constraint(v, pltpu.HBM) for v in (spectra, travel)))
    by_row = [from_offset(payload, "srow", d) for d in (1, 2, 3)]
    by_col = [from_offset(payload, "scol", d) for d in ROW_OFF[1:]]
    steer0 = steer(bins, [payload])
    steer2 = steer(bins, by_row)
    by_col, steer0, steer2 = lax.optimization_barrier((by_col, steer0, steer2))
    a0 = stack([payload] + by_row + by_col)
    a1 = from_partner(a0, 2)
    a2 = from_partner(a0, 1)
    steer1 = steer(bins, by_col)
    a1, steer1 = lax.optimization_barrier((a1, steer1))
    a3 = from_partner(a1, 1)
    sources = (a0, a1, a2, a3)
    packed = pack(sources)
    rows = from_offset(packed, "scol", 2)
    partial = beams(steer0, steer1, steer2, sources)
    shares = lax.all_to_all(partial.reshape(128, 4, NST), ALL, 0, 0, tiled=True)
    coherence = far_tile(rows, sources, near_tile(sources))
    beam = shares.reshape(4, 32, 4, NST).sum(axis=1).reshape(1, 4 * NPT)
    return coherence.reshape(1, 2, 1024, 4, NST), beam


def solution(mesh):
    placed = (P(None, None, "win", ("srow", "scol")), P(), P(("srow", "scol"), "win"))
    return jax.shard_map(
        local,
        mesh=mesh,
        in_specs=placed,
        out_specs=(P("win", None, "srow", None, "scol"), P("win", None)),
        check_vma=False,
    )
```

```python
import jax
import jax.numpy as jnp
from jax import lax
from jax.experimental import pallas as pl
from jax.experimental.pallas import tpu as pltpu
from jax.sharding import PartitionSpec as P

S = 4096
NFFT = 4096
F = 4
NST = 128
NPT = 512
ALL = ("win", "srow", "scol")
ROW_OFF = (0, 1, 2, -3, 4)
WEIGHT = ((1, 2, 1), (2, 2, 2, 2), (2, 2, 2, 2), (2, 2, 2, 2), (1, 2, 1))
RELAY = (4, 6, 7)
ROUND = 12582912.0

ROOT2 = 2.0**0.5
SIN = [ROOT2 * v for v in (3.141592580044453, -5.167706878911761, 2.5500313770692338,
                           -0.5980451729935192, 0.07722012694435497)]
COS = [-ROOT2 * v for v in (0.9999999534664096, -4.93479285864205, 4.058411913501759,
                            -1.331880156986464, 0.2196967900729894)]


def prep_kernel(spectra_hbm, travel_hbm, bins_hbm, payload, scales, spectra, travel, bins, sems):
    moves = [
        pltpu.make_async_copy(spectra_hbm, spectra, sems.at[0]),
        pltpu.make_async_copy(travel_hbm, travel, sems.at[1]),
        pltpu.make_async_copy(bins_hbm, bins, sems.at[2]),
    ]
    for move in moves:
        move.start()
    moves[0].wait()
    for f in range(F):
        re = spectra[f, 0]
        im = spectra[f, 1]
        magnitude = jnp.sqrt(re * re + im * im + 0.5)
        for c, part in enumerate((re, im)):
            value = (part / magnitude).astype(jnp.bfloat16).astype(jnp.float32) * 32768.0
            value = jnp.clip((value + ROUND) - ROUND, -32767.0, 32767.0)
            at = NPT + 32 * f + 16 * c
            payload[at:at + 16, :] = value.astype(jnp.int32).astype(jnp.int16)
    moves[1].wait()
    payload[0:NPT, :] = travel[...].T.astype(jnp.int16)
    moves[2].wait()
    for f in range(F):
        scales[f] = jnp.full((8, NST), bins[f].astype(jnp.float32) * (1.0 / NFFT), jnp.float32)


def on_chip(*arrays):
    return [pltpu.with_memory_space_constraint(v, pltpu.VMEM) for v in arrays]


def vmem(n):
    return [pl.BlockSpec(memory_space=pltpu.VMEM)] * n


SMEM = pl.BlockSpec(memory_space=pltpu.SMEM)
LIMIT = pltpu.CompilerParams(vmem_limit_bytes=16 * 2**20)


def steer_kernel(scales, *refs):
    payloads, out = refs[:-1], refs[-1]
    rows = 64
    for n, ref in enumerate(payloads):
        def chunk(i, carry, n=n, ref=ref):
            at = pl.ds(pl.multiple_of(i * rows, rows), rows)
            samples = (ref[at, :].astype(jnp.int32) & (NFFT - 1)).astype(jnp.float32)
            for f in range(F):
                turns = (samples.reshape(rows // 8, 8, NST) * scales[f]).reshape(rows, NST)
                r = turns - ((turns + ROUND) - ROUND)
                z = r * r
                s = SIN[4]
                c = COS[4]
                for k in (3, 2, 1, 0):
                    s = s * z + SIN[k]
                    c = c * z + COS[k]
                s = s * r
                out[f, 0, n, at, :] = (1.0 - s * s).astype(jnp.bfloat16)
                out[f, 1, n, at, :] = (s * c).astype(jnp.bfloat16)
            return carry

        lax.fori_loop(0, NPT // rows, chunk, 0)


def steer(scales, payloads):
    n = len(payloads)
    return pl.pallas_call(
        steer_kernel,
        out_shape=pltpu.VMEM((F, 2, n, NPT, NST), jnp.bfloat16),
        in_specs=vmem(n + 1),
        out_specs=vmem(1)[0],
        compiler_params=LIMIT,
    )(*on_chip(scales, *payloads))


def stack_kernel(*refs):
    for n, ref in enumerate(refs[:-1]):
        refs[-1][n] = ref[NPT:NPT + 32 * F, :]


def stack(payloads):
    return pl.pallas_call(
        stack_kernel,
        out_shape=pltpu.VMEM((len(payloads), 32 * F, NST), jnp.int16),
        in_specs=vmem(len(payloads)),
        out_specs=vmem(1)[0],
        compiler_params=LIMIT,
        name="stack",
    )(*on_chip(*payloads))


def decode(sources, block, f):
    at = slice(32 * f, 32 * f + 32) if isinstance(f, int) else pl.ds(pl.multiple_of(32 * f, 32), 32)
    return [
        (a[block, at, :].astype(jnp.int32).astype(jnp.float32) * (1.0 / 32768.0)).astype(jnp.bfloat16)
        for a in sources
    ]


def beam_kernel(own_steer, col_steer, row_steer, a0, a1, a2, a3, beam, cols, weights):
    sources = (a0, a1, a2, a3)

    def one(f, carry):
        for d in range(4):
            cols[d * NST:(d + 1) * NST, :] = jnp.concatenate(decode(sources, d, f), axis=0).T

        def coherent(k):
            parts = decode(sources, 0 if k == 0 else 3 + k, f)
            x = jnp.concatenate(parts, axis=0)
            z = jnp.concatenate([q for v in parts for q in (v[16:32], -v[0:16])], axis=0)
            right = jnp.concatenate([x, z], axis=1)
            for j, weight in enumerate(WEIGHT[k]):
                at = slice(j * NST, (j + 1) * NST)
                cross = jnp.dot(cols[at, :], right, preferred_element_type=jnp.float32)
                re = cross[:, :NST]
                im = cross[:, NST:]
                inverse = lax.rsqrt(re * re + im * im + 64.0)
                if weight == 2:
                    inverse = inverse + inverse
                re = (re * inverse).astype(jnp.bfloat16)
                im = (im * inverse).astype(jnp.bfloat16)
                at = slice(2 * j * NST, (2 * j + 1) * NST)
                weights[k, at, :NST] = re
                weights[k, at, NST:] = im
                at = slice((2 * j + 1) * NST, (2 * j + 2) * NST)
                weights[k, at, :NST] = -im
                weights[k, at, NST:] = re

        steer_cols = jnp.concatenate(
            [own_steer[f, 0, 0], own_steer[f, 1, 0]] + [row_steer[f, part, n] for n in range(3) for part in range(2)],
            axis=1,
        )
        total = None
        coherent(0)
        for k in range(5):
            if k < 4:
                coherent(k + 1)
            depth = 2 * NST * len(WEIGHT[k])
            image = jnp.dot(steer_cols[:, :depth], weights[k, :depth], preferred_element_type=jnp.float32)
            re, im = (own_steer[f, 0, 0], own_steer[f, 1, 0]) if k == 0 else (col_steer[f, 0, k - 1], col_steer[f, 1, k - 1])
            power = re.astype(jnp.float32) * image[:, :NST] + im.astype(jnp.float32) * image[:, NST:]
            total = power if total is None else total + power
        values = []
        for j in range(4):
            value = jnp.sum(total[j * NST:(j + 1) * NST, :].T, axis=0, keepdims=True) * (1.0 / S)
            values.append(value)
        beam[f] = jnp.broadcast_to(jnp.concatenate(values, axis=0)[None], (32, 4, NST)).astype(jnp.bfloat16)
        return carry

    for f in range(F):
        one(f, 0)


def beams(own_steer, col_steer, row_steer, spectra):
    return pl.pallas_call(
        beam_kernel,
        out_shape=pltpu.VMEM((F, 32, 4, NST), jnp.bfloat16),
        in_specs=vmem(7),
        out_specs=vmem(1)[0],
        scratch_shapes=[
            pltpu.VMEM((4 * NST, NST), jnp.bfloat16),
            pltpu.VMEM((5, 8 * NST, 2 * NST), jnp.bfloat16),
        ],
        compiler_params=LIMIT,
        name="beams",
    )(*on_chip(own_steer, col_steer, row_steer, *spectra))


def pack_kernel(a0, a1, a2, a3, rows):
    at = pl.ds(pl.multiple_of(32 * lax.axis_index("win"), 32), 32)
    for s, a in enumerate((a0, a1, a2, a3)):
        for n, block in enumerate(RELAY):
            rows[s, n] = a[block, at, :]


def pack(spectra):
    return pl.pallas_call(
        pack_kernel,
        out_shape=pltpu.VMEM((4, 3, 32, NST), jnp.int16),
        in_specs=vmem(4),
        out_specs=vmem(1)[0],
        compiler_params=LIMIT,
        name="pack",
    )(*on_chip(*spectra))


def fill_columns(sources, f, cols):
    for d in range(4):
        parts = decode(sources, d, f)
        x = jnp.concatenate(parts, axis=0)
        y = jnp.concatenate([q for v in parts for q in (-v[16:32], v[0:16])], axis=0)
        cols[d] = jnp.concatenate([x, y], axis=1)


def emit(parts, cols, r, scratch, ready):
    left = jnp.concatenate(parts, axis=0).T
    for d in range(4):
        cross = jnp.dot(left, cols[d], preferred_element_type=jnp.float32)
        re = cross[:, :NST]
        im = cross[:, NST:]
        inverse = lax.rsqrt(re * re + im * im + 64.0)
        at = pl.ds((r + d) & 3, NST, stride=4)
        scratch[0, at, :] = re * inverse
        scratch[1, at, :] = im * inverse
    ready[0] = scratch[0].astype(jnp.bfloat16)
    ready[1] = scratch[1].astype(jnp.bfloat16)


def block_copy(ready, coherence, offset, sem):
    row = (lax.axis_index("scol") + offset) & 7
    at = pl.ds(pl.multiple_of(row * (4 * NST), 4 * NST), 4 * NST)
    return pltpu.make_async_copy(ready, coherence.at[:, at, :], sem)


def near_kernel(a0, a1, a2, a3, coherence, cols, scratch, ready, sems):
    w, r = lax.axis_index("win"), lax.axis_index("srow")
    sources = (a0, a1, a2, a3)
    fill_columns(sources, w, cols)
    for n, offset in enumerate(ROW_OFF):
        emit(decode(sources, 0 if n == 0 else 3 + n, w), cols, r, scratch, ready.at[n])
        block_copy(ready.at[n], coherence, offset, sems.at[n]).start()
    for n, offset in enumerate(ROW_OFF):
        block_copy(ready.at[n], coherence, offset, sems.at[n]).wait()


def far_kernel(rows, a0, a1, a2, a3, old, coherence, cols, scratch, ready, sems):
    w, r = lax.axis_index("win"), lax.axis_index("srow")
    fill_columns((a0, a1, a2, a3), w, cols)
    for n, offset in enumerate((3, -1, -2)):
        emit(decode([rows.at[k] for k in range(4)], n, 0), cols, r, scratch, ready.at[n])
        block_copy(ready.at[n], coherence, offset, sems.at[n]).start()
    for n, offset in enumerate((3, -1, -2)):
        block_copy(ready.at[n], coherence, offset, sems.at[n]).wait()


def tile_scratch(n):
    return [
        pltpu.VMEM((4, NST, 2 * NST), jnp.bfloat16),
        pltpu.VMEM((2, 4 * NST, NST), jnp.float32),
        pltpu.VMEM((n, 2, 4 * NST, NST), jnp.bfloat16),
        pltpu.SemaphoreType.DMA((n,)),
    ]


TILE = jax.ShapeDtypeStruct((2, 4 * 1024, NST), jnp.bfloat16)
ANY = pl.BlockSpec(memory_space=pl.ANY)


def near_tile(spectra):
    return pl.pallas_call(
        near_kernel,
        in_specs=vmem(4),
        out_specs=ANY,
        scratch_shapes=tile_scratch(5),
        out_shape=TILE,
        compiler_params=LIMIT,
        name="near",
    )(*on_chip(*spectra))


def far_tile(rows, spectra, coherence):
    return pl.pallas_call(
        far_kernel,
        in_specs=vmem(5) + [ANY],
        out_specs=ANY,
        scratch_shapes=tile_scratch(3),
        out_shape=TILE,
        input_output_aliases={5: 0},
        compiler_params=LIMIT,
        name="far",
    )(*on_chip(rows, *spectra), coherence)


def from_offset(value, axis, offset):
    size = lax.axis_size(axis)
    return lax.ppermute(value, axis, [((i + offset) % size, i) for i in range(size)])


def from_partner(value, bit):
    return lax.ppermute(value, "win", [(i ^ bit, i) for i in range(4)])


def local(spectra, bins, travel):
    payload, scales = pl.pallas_call(
        prep_kernel,
        out_shape=(
            pltpu.VMEM((NPT + 32 * F, NST), jnp.int16),
            pltpu.VMEM((F, 8, NST), jnp.float32),
        ),
        in_specs=[ANY] * 3,
        out_specs=tuple(vmem(2)),
        scratch_shapes=[
            pltpu.VMEM(spectra.shape, jnp.float32),
            pltpu.VMEM(travel.shape, jnp.int32),
            pltpu.SMEM((F,), jnp.int32),
            pltpu.SemaphoreType.DMA((3,)),
        ],
        compiler_params=LIMIT,
        name="prep",
    )(*(pltpu.with_memory_space_constraint(v, pltpu.HBM) for v in (spectra, travel, bins)))
    by_row = [from_offset(payload, "srow", d) for d in (1, 2, 3)]
    by_col = [from_offset(payload, "scol", d) for d in ROW_OFF[1:]]
    steer0 = steer(scales, [payload])
    steer2 = steer(scales, by_row)
    by_col, steer0, steer2 = lax.optimization_barrier((by_col, steer0, steer2))
    a0 = stack([payload] + by_row + by_col)
    a1 = from_partner(a0, 2)
    a2 = from_partner(a0, 1)
    steer1 = steer(scales, by_col)
    a1, steer1 = lax.optimization_barrier((a1, steer1))
    a3 = from_partner(a1, 1)
    sources = (a0, a1, a2, a3)
    packed = pack(sources)
    rows = from_offset(packed, "scol", 2)
    partial = beams(steer0, steer1, steer2, sources)
    shares = lax.all_to_all(partial.reshape(128, 4, NST), ALL, 0, 0, tiled=True)
    coherence = far_tile(rows, sources, near_tile(sources))
    beam = shares.astype(jnp.float32).reshape(4, 32, 4, NST).sum(axis=1).reshape(1, 4 * NPT)
    return coherence.reshape(1, 2, 1024, 4, NST), beam


def solution(mesh):
    placed = (P(None, None, "win", ("srow", "scol")), P(), P(("srow", "scol"), "win"))
    return jax.shard_map(
        local,
        mesh=mesh,
        in_specs=placed,
        out_specs=(P("win", None, "srow", None, "scol"), P("win", None)),
        check_vma=False,
    )
```

```python
import jax
import jax.numpy as jnp
from jax import lax
from jax.experimental import pallas as pl
from jax.experimental.pallas import tpu as pltpu
from jax.sharding import PartitionSpec as P


S = 4096
NFFT = 4096
F = 4
NST = 128
NPT = 512
ALL = ("win", "srow", "scol")
ROW_OFF = (0, 1, 2, -3, 4)
WEIGHT = ((1, 2, 1), (2, 2, 2, 2), (2, 2, 2, 2), (2, 2, 2, 2), (1, 2, 1))
RELAY = (4, 6, 7)
SENDS = (('srow', 3), ('srow', 2), ('scol', 2), ('srow', 1), ('scol', 4), ('scol', -3), ('scol', 1))
ROUND = 12582912.0
AHEAD = 1

ROOT2 = 2.0**0.5
SIN = [ROOT2 * v for v in (3.141592580044453, -5.167706878911761, 2.5500313770692338,
                           -0.5980451729935192, 0.07722012694435497)]
COS = [-ROOT2 * v for v in (0.9999999534664096, -4.93479285864205, 4.058411913501759,
                            -1.331880156986464, 0.2196967900729894)]


def prep_kernel(spectra_hbm, travel_hbm, bins_hbm, payload, scales, spectra, travel, bins, sems):
    moves = [
        pltpu.make_async_copy(spectra_hbm, spectra, sems.at[0]),
        pltpu.make_async_copy(travel_hbm, travel, sems.at[1]),
        pltpu.make_async_copy(bins_hbm, bins, sems.at[2]),
    ]
    for move in moves:
        move.start()
    moves[0].wait()
    for f in range(F):
        re = spectra[f, 0]
        im = spectra[f, 1]
        magnitude = jnp.sqrt(re * re + im * im + 0.5)
        for c, part in enumerate((re, im)):
            value = (part / magnitude).astype(jnp.bfloat16).astype(jnp.float32) * 32768.0
            value = jnp.clip((value + ROUND) - ROUND, -32767.0, 32767.0)
            at = NPT + 32 * f + 16 * c
            payload[at:at + 16, :] = value.astype(jnp.int32).astype(jnp.int16)
    moves[1].wait()
    payload[0:NPT, :] = travel[...].T.astype(jnp.int16)
    moves[2].wait()
    for f in range(F):
        scales[f] = jnp.full((8, NST), bins[f].astype(jnp.float32) * (1.0 / NFFT), jnp.float32)


def on_chip(*arrays):
    return [pltpu.with_memory_space_constraint(v, pltpu.VMEM) for v in arrays]


def vmem(n):
    return [pl.BlockSpec(memory_space=pltpu.VMEM)] * n


SMEM = pl.BlockSpec(memory_space=pltpu.SMEM)
LIMIT = pltpu.CompilerParams(vmem_limit_bytes=16 * 2**20)


def steer_kernel(scales, *refs):
    payloads, out = refs[:-1], refs[-1]
    rows = 64
    for n, ref in enumerate(payloads):
        def chunk(i, carry, n=n, ref=ref):
            at = pl.ds(pl.multiple_of(i * rows, rows), rows)
            samples = (ref[at, :].astype(jnp.int32) & (NFFT - 1)).astype(jnp.float32)
            for f in range(F):
                turns = (samples.reshape(rows // 8, 8, NST) * scales[f]).reshape(rows, NST)
                r = turns - lax.round(turns, lax.RoundingMethod.TO_NEAREST_EVEN)
                z = r * r
                s = SIN[4]
                c = COS[4]
                for k in (3, 2, 1, 0):
                    s = s * z + SIN[k]
                    c = c * z + COS[k]
                s = s * r
                out[f, 0, n, at, :] = (1.0 - s * s).astype(jnp.bfloat16)
                out[f, 1, n, at, :] = (s * c).astype(jnp.bfloat16)
            return carry

        lax.fori_loop(0, NPT // rows, chunk, 0)


def steer(scales, payloads):
    n = len(payloads)
    return pl.pallas_call(
        steer_kernel,
        out_shape=pltpu.VMEM((F, 2, n, NPT, NST), jnp.bfloat16),
        in_specs=vmem(n + 1),
        out_specs=vmem(1)[0],
        compiler_params=LIMIT,
    )(*on_chip(scales, *payloads))


def stack_kernel(*refs):
    for n, ref in enumerate(refs[:-1]):
        refs[-1][n] = ref[NPT:NPT + 32 * F, :]


def stack(payloads):
    return pl.pallas_call(
        stack_kernel,
        out_shape=pltpu.VMEM((len(payloads), 32 * F, NST), jnp.int16),
        in_specs=vmem(len(payloads)),
        out_specs=vmem(1)[0],
        compiler_params=LIMIT,
        name="stack",
    )(*on_chip(*payloads))


def decode(sources, block, f):
    at = slice(32 * f, 32 * f + 32) if isinstance(f, int) else pl.ds(pl.multiple_of(32 * f, 32), 32)
    return [
        (a[block, at, :].astype(jnp.int32).astype(jnp.float32) * (1.0 / 32768.0)).astype(jnp.bfloat16)
        for a in sources
    ]


def beam_kernel(own_steer, col_steer, row_steer, a0, a1, a2, a3, beam, cols, weights):
    sources = (a0, a1, a2, a3)

    def coherent(f, k):
        if k == 0:
            for d in range(4):
                cols[f % 2, d * NST:(d + 1) * NST, :] = jnp.concatenate(decode(sources, d, f), axis=0).T
        parts = decode(sources, 0 if k == 0 else 3 + k, f)
        x = jnp.concatenate(parts, axis=0)
        z = jnp.concatenate([q for v in parts for q in (v[16:32], -v[0:16])], axis=0)
        right = jnp.concatenate([x, z], axis=1)
        for j, weight in enumerate(WEIGHT[k]):
            at = slice(j * NST, (j + 1) * NST)
            cross = jnp.dot(cols[f % 2, at, :], right, preferred_element_type=jnp.float32)
            re = cross[:, :NST]
            im = cross[:, NST:]
            inverse = lax.rsqrt(re * re + im * im + 64.0)
            if weight == 2:
                inverse = inverse + inverse
            re = (re * inverse).astype(jnp.bfloat16)
            im = (im * inverse).astype(jnp.bfloat16)
            at = slice(2 * j * NST, (2 * j + 1) * NST)
            weights[k, at, :NST] = re
            weights[k, at, NST:] = im
            at = slice((2 * j + 1) * NST, (2 * j + 2) * NST)
            weights[k, at, :NST] = -im
            weights[k, at, NST:] = re

    def product(f, k):
        depth = len(WEIGHT[k])
        steer_cols = jnp.concatenate(
            ([own_steer[f, 0, 0], own_steer[f, 1, 0]] + [row_steer[f, part, n] for n in range(3) for part in range(2)])[:2 * depth],
            axis=1,
        )
        image = jnp.dot(steer_cols, weights[k, :2 * NST * depth], preferred_element_type=jnp.float32)
        re, im = (own_steer[f, 0, 0], own_steer[f, 1, 0]) if k == 0 else (col_steer[f, 0, k - 1], col_steer[f, 1, k - 1])
        return re.astype(jnp.float32) * image[:, :NST] + im.astype(jnp.float32) * image[:, NST:]

    steps = [(f, k) for f in range(F) for k in range(5)]
    for step in steps[:AHEAD]:
        coherent(*step)
    for n, (f, k) in enumerate(steps):
        if n + AHEAD < len(steps):
            coherent(*steps[n + AHEAD])
        power = product(f, k)
        total = power if k == 0 else total + power
        if k == 4:
            values = [
                jnp.sum(total[j * NST:(j + 1) * NST, :].T, axis=0, keepdims=True) * (1.0 / S) for j in range(4)
            ]
            beam[f] = jnp.broadcast_to(jnp.concatenate(values, axis=0)[None], (32, 4, NST)).astype(jnp.bfloat16)


def beams(own_steer, col_steer, row_steer, spectra):
    return pl.pallas_call(
        beam_kernel,
        out_shape=pltpu.VMEM((F, 32, 4, NST), jnp.bfloat16),
        in_specs=vmem(7),
        out_specs=vmem(1)[0],
        scratch_shapes=[
            pltpu.VMEM((2, 4 * NST, NST), jnp.bfloat16),
            pltpu.VMEM((5, 8 * NST, 2 * NST), jnp.bfloat16),
        ],
        compiler_params=LIMIT,
        name="beams",
    )(*on_chip(own_steer, col_steer, row_steer, *spectra))


def pack_kernel(a0, a1, a2, a3, rows):
    at = pl.ds(pl.multiple_of(32 * lax.axis_index("win"), 32), 32)
    for s, a in enumerate((a0, a1, a2, a3)):
        for n, block in enumerate(RELAY):
            rows[s, n] = a[block, at, :]


def pack(spectra):
    return pl.pallas_call(
        pack_kernel,
        out_shape=pltpu.VMEM((4, 3, 32, NST), jnp.int16),
        in_specs=vmem(4),
        out_specs=vmem(1)[0],
        compiler_params=LIMIT,
        name="pack",
    )(*on_chip(*spectra))


def fill_columns(sources, f, cols):
    for d in range(4):
        parts = decode(sources, d, f)
        x = jnp.concatenate(parts, axis=0)
        y = jnp.concatenate([q for v in parts for q in (-v[16:32], v[0:16])], axis=0)
        cols[d] = jnp.concatenate([x, y], axis=1)


def emit(parts, cols, r, scratch, ready):
    left = jnp.concatenate(parts, axis=0).T
    for d in range(4):
        cross = jnp.dot(left, cols[d], preferred_element_type=jnp.float32)
        re = cross[:, :NST]
        im = cross[:, NST:]
        inverse = lax.rsqrt(re * re + im * im + 64.0)
        at = pl.ds((r + d) & 3, NST, stride=4)
        scratch[0, at, :] = re * inverse
        scratch[1, at, :] = im * inverse
    ready[0] = scratch[0].astype(jnp.bfloat16)
    ready[1] = scratch[1].astype(jnp.bfloat16)


def block_copy(ready, coherence, offset, sem):
    row = (lax.axis_index("scol") + offset) & 7
    at = pl.ds(pl.multiple_of(row * (4 * NST), 4 * NST), 4 * NST)
    return pltpu.make_async_copy(ready, coherence.at[:, at, :], sem)


def near_kernel(a0, a1, a2, a3, coherence, cols, scratch, ready, sems):
    w, r = lax.axis_index("win"), lax.axis_index("srow")
    sources = (a0, a1, a2, a3)
    fill_columns(sources, w, cols)
    for n, offset in enumerate(ROW_OFF):
        emit(decode(sources, 0 if n == 0 else 3 + n, w), cols, r, scratch, ready.at[n])
        block_copy(ready.at[n], coherence, offset, sems.at[n]).start()
    for n, offset in enumerate(ROW_OFF):
        block_copy(ready.at[n], coherence, offset, sems.at[n]).wait()


def far_kernel(rows, a0, a1, a2, a3, old, coherence, cols, scratch, ready, sems):
    w, r = lax.axis_index("win"), lax.axis_index("srow")
    fill_columns((a0, a1, a2, a3), w, cols)
    for n, offset in enumerate((3, -1, -2)):
        emit(decode([rows.at[k] for k in range(4)], n, 0), cols, r, scratch, ready.at[n])
        block_copy(ready.at[n], coherence, offset, sems.at[n]).start()
    for n, offset in enumerate((3, -1, -2)):
        block_copy(ready.at[n], coherence, offset, sems.at[n]).wait()


def tile_scratch(n):
    return [
        pltpu.VMEM((4, NST, 2 * NST), jnp.bfloat16),
        pltpu.VMEM((2, 4 * NST, NST), jnp.float32),
        pltpu.VMEM((n, 2, 4 * NST, NST), jnp.bfloat16),
        pltpu.SemaphoreType.DMA((n,)),
    ]


TILE = jax.ShapeDtypeStruct((2, 4 * 1024, NST), jnp.bfloat16)
ANY = pl.BlockSpec(memory_space=pl.ANY)


def near_tile(spectra):
    return pl.pallas_call(
        near_kernel,
        in_specs=vmem(4),
        out_specs=ANY,
        scratch_shapes=tile_scratch(5),
        out_shape=TILE,
        compiler_params=LIMIT,
        name="near",
    )(*on_chip(*spectra))


def far_tile(rows, spectra, coherence):
    return pl.pallas_call(
        far_kernel,
        in_specs=vmem(5) + [ANY],
        out_specs=ANY,
        scratch_shapes=tile_scratch(3),
        out_shape=TILE,
        input_output_aliases={5: 0},
        compiler_params=LIMIT,
        name="far",
    )(*on_chip(rows, *spectra), coherence)


def from_offset(value, axis, offset):
    size = lax.axis_size(axis)
    return lax.ppermute(value, axis, [((i + offset) % size, i) for i in range(size)])


def from_partner(value, bit):
    return lax.ppermute(value, "win", [(i ^ bit, i) for i in range(4)])


def body(spectra, bins, travel):
    return local(spectra, bins, travel)


def local(spectra, bins, travel):
    return local(spectra, bins, travel)


def local(spectra, bins, travel):
    payload, scales = pl.pallas_call(
        prep_kernel,
        out_shape=(
            pltpu.VMEM((NPT + 32 * F, NST), jnp.int16),
            pltpu.VMEM((F, 8, NST), jnp.float32),
        ),
        in_specs=[ANY] * 3,
        out_specs=tuple(vmem(2)),
        scratch_shapes=[
            pltpu.VMEM(spectra.shape, jnp.float32),
            pltpu.VMEM(travel.shape, jnp.int32),
            pltpu.SMEM((F,), jnp.int32),
            pltpu.SemaphoreType.DMA((3,)),
        ],
        compiler_params=LIMIT,
        name="prep",
    )(*(pltpu.with_memory_space_constraint(v, pltpu.HBM) for v in (spectra, travel, bins)))
    got = {}
    for axis, offset in SENDS:
        got[axis, offset] = from_offset(payload, axis, offset)
    by_row = [got["srow", d] for d in (1, 2, 3)]
    by_col = [got["scol", d] for d in ROW_OFF[1:]]
    steer0 = steer(scales, [payload])
    steer2 = steer(scales, by_row)
    by_col, steer0, steer2 = lax.optimization_barrier((by_col, steer0, steer2))
    a0 = stack([payload] + by_row + by_col)
    a1 = from_partner(a0, 2)
    steer1 = steer(scales, by_col)
    a0, steer1 = lax.optimization_barrier((a0, steer1))
    a2 = from_partner(a0, 1)
    a1, steer1 = lax.optimization_barrier((a1, steer1))
    a3 = from_partner(a1, 1)
    sources = (a0, a1, a2, a3)
    packed = pack(sources)
    rows = from_offset(packed, "scol", 2)
    partial = beams(steer0, steer1, steer2, sources)
    shares = lax.all_to_all(partial.reshape(128, 4, NST), ALL, 0, 0, tiled=True)
    coherence = far_tile(rows, sources, near_tile(sources))
    beam = shares.astype(jnp.float32).reshape(4, 32, 4, NST).sum(axis=1).reshape(1, 4 * NPT)
    return coherence.reshape(1, 2, 1024, 4, NST), beam


def solution(mesh):
    placed = (P(None, None, "win", ("srow", "scol")), P(), P(("srow", "scol"), "win"))
    return jax.shard_map(
        body,
        mesh=mesh,
        in_specs=placed,
        out_specs=(P("win", None, "srow", None, "scol"), P("win", None)),
        check_vma=False,
    )
```

```python
import jax
import jax.numpy as jnp
from jax import lax
from jax.experimental import pallas as pl
from jax.experimental.pallas import tpu as pltpu
from jax.sharding import PartitionSpec as P


S = 4096
NFFT = 4096
F = 4
NST = 128
NPT = 512
ALL = ("win", "srow", "scol")
ROW_OFF = (0, 1, 2, -3, 4)
WEIGHT = ((1, 2, 1), (2, 2, 2, 2), (2, 2, 2, 2), (2, 2, 2, 2), (1, 2, 1))
RELAY = (4, 6, 7)
SENDS = (('srow', 3), ('srow', 2), ('srow', 1), ('scol', 2), ('scol', 4), ('scol', -3), ('scol', 1))
ROUND = 12582912.0
AHEAD = 1

ROOT2 = 2.0**0.5
SIN = [ROOT2 * v for v in (3.141592580044453, -5.167706878911761, 2.5500313770692338,
                           -0.5980451729935192, 0.07722012694435497)]
COS = [-ROOT2 * v for v in (0.9999999534664096, -4.93479285864205, 4.058411913501759,
                            -1.331880156986464, 0.2196967900729894)]


def prep_kernel(spectra_hbm, travel_hbm, bins_hbm, payload, scales, spectra, travel, bins, sems):
    moves = [
        pltpu.make_async_copy(spectra_hbm, spectra, sems.at[0]),
        pltpu.make_async_copy(travel_hbm, travel, sems.at[1]),
        pltpu.make_async_copy(bins_hbm, bins, sems.at[2]),
    ]
    for move in moves:
        move.start()
    moves[0].wait()
    for f in range(F):
        re = spectra[f, 0]
        im = spectra[f, 1]
        magnitude = jnp.sqrt(re * re + im * im + 0.5)
        for c, part in enumerate((re, im)):
            value = (part / magnitude).astype(jnp.bfloat16).astype(jnp.float32) * 32768.0
            value = jnp.clip((value + ROUND) - ROUND, -32767.0, 32767.0)
            at = NPT + 32 * f + 16 * c
            payload[at:at + 16, :] = value.astype(jnp.int32).astype(jnp.int16)
    moves[1].wait()
    payload[0:NPT, :] = travel[...].T.astype(jnp.int16)
    moves[2].wait()
    for f in range(F):
        scales[f] = jnp.full((8, NST), bins[f].astype(jnp.float32) * (1.0 / NFFT), jnp.float32)


def on_chip(*arrays):
    return [pltpu.with_memory_space_constraint(v, pltpu.VMEM) for v in arrays]


def vmem(n):
    return [pl.BlockSpec(memory_space=pltpu.VMEM)] * n


SMEM = pl.BlockSpec(memory_space=pltpu.SMEM)
LIMIT = pltpu.CompilerParams(vmem_limit_bytes=16 * 2**20)


def steer_kernel(scales, *refs):
    payloads, out = refs[:-1], refs[-1]
    rows = 64
    for n, ref in enumerate(payloads):
        def chunk(i, carry, n=n, ref=ref):
            at = pl.ds(pl.multiple_of(i * rows, rows), rows)
            samples = (ref[at, :].astype(jnp.int32) & (NFFT - 1)).astype(jnp.float32)
            for f in range(F):
                turns = (samples.reshape(rows // 8, 8, NST) * scales[f]).reshape(rows, NST)
                r = turns - lax.round(turns, lax.RoundingMethod.TO_NEAREST_EVEN)
                z = r * r
                s = SIN[4]
                c = COS[4]
                for k in (3, 2, 1, 0):
                    s = s * z + SIN[k]
                    c = c * z + COS[k]
                s = s * r
                out[f, 0, n, at, :] = (1.0 - s * s).astype(jnp.bfloat16)
                out[f, 1, n, at, :] = (s * c).astype(jnp.bfloat16)
            return carry

        lax.fori_loop(0, NPT // rows, chunk, 0)


def steer(scales, payloads):
    n = len(payloads)
    return pl.pallas_call(
        steer_kernel,
        out_shape=pltpu.VMEM((F, 2, n, NPT, NST), jnp.bfloat16),
        in_specs=vmem(n + 1),
        out_specs=vmem(1)[0],
        compiler_params=LIMIT,
    )(*on_chip(scales, *payloads))


def stack_kernel(*refs):
    for n, ref in enumerate(refs[:-1]):
        refs[-1][n] = ref[NPT:NPT + 32 * F, :]


def stack(payloads):
    return pl.pallas_call(
        stack_kernel,
        out_shape=pltpu.VMEM((len(payloads), 32 * F, NST), jnp.int16),
        in_specs=vmem(len(payloads)),
        out_specs=vmem(1)[0],
        compiler_params=LIMIT,
        name="stack",
    )(*on_chip(*payloads))


def decode(sources, block, f):
    at = slice(32 * f, 32 * f + 32) if isinstance(f, int) else pl.ds(pl.multiple_of(32 * f, 32), 32)
    return [
        (a[block, at, :].astype(jnp.int32).astype(jnp.float32) * (1.0 / 32768.0)).astype(jnp.bfloat16)
        for a in sources
    ]


def beam_kernel(own_steer, col_steer, row_steer, a0, a1, a2, a3, beam, cols, weights):
    sources = (a0, a1, a2, a3)

    def coherent(f, k):
        if k == 0:
            for d in range(4):
                cols[f % 2, d * NST:(d + 1) * NST, :] = jnp.concatenate(decode(sources, d, f), axis=0).T
        parts = decode(sources, 0 if k == 0 else 3 + k, f)
        x = jnp.concatenate(parts, axis=0)
        z = jnp.concatenate([q for v in parts for q in (v[16:32], -v[0:16])], axis=0)
        right = jnp.concatenate([x, z], axis=1)
        whole = jnp.dot(cols[f % 2, :len(WEIGHT[k]) * NST, :], right, preferred_element_type=jnp.float32)
        for j, weight in enumerate(WEIGHT[k]):
            cross = whole[j * NST:(j + 1) * NST]
            re = cross[:, :NST]
            im = cross[:, NST:]
            inverse = lax.rsqrt(re * re + im * im + 64.0)
            if weight == 2:
                inverse = inverse + inverse
            re = (re * inverse).astype(jnp.bfloat16)
            im = (im * inverse).astype(jnp.bfloat16)
            at = slice(2 * j * NST, (2 * j + 1) * NST)
            weights[k, at, :NST] = re
            weights[k, at, NST:] = im
            at = slice((2 * j + 1) * NST, (2 * j + 2) * NST)
            weights[k, at, :NST] = -im
            weights[k, at, NST:] = re

    def product(f, k):
        depth = len(WEIGHT[k])
        steer_cols = jnp.concatenate(
            ([own_steer[f, 0, 0], own_steer[f, 1, 0]] + [row_steer[f, part, n] for n in range(3) for part in range(2)])[:2 * depth],
            axis=1,
        )
        image = jnp.dot(steer_cols, weights[k, :2 * NST * depth], preferred_element_type=jnp.float32)
        re, im = (own_steer[f, 0, 0], own_steer[f, 1, 0]) if k == 0 else (col_steer[f, 0, k - 1], col_steer[f, 1, k - 1])
        return re.astype(jnp.float32) * image[:, :NST] + im.astype(jnp.float32) * image[:, NST:]

    steps = [(f, k) for f in range(F) for k in range(5)]
    for step in steps[:AHEAD]:
        coherent(*step)
    for n, (f, k) in enumerate(steps):
        if n + AHEAD < len(steps):
            coherent(*steps[n + AHEAD])
        power = product(f, k)
        total = power if k == 0 else total + power
        if k == 4:
            values = [
                jnp.sum(total[j * NST:(j + 1) * NST, :].T, axis=0, keepdims=True) * (1.0 / S) for j in range(4)
            ]
            beam[f] = jnp.broadcast_to(jnp.concatenate(values, axis=0)[None], (32, 4, NST)).astype(jnp.bfloat16)


def beams(own_steer, col_steer, row_steer, spectra):
    return pl.pallas_call(
        beam_kernel,
        out_shape=pltpu.VMEM((F, 32, 4, NST), jnp.bfloat16),
        in_specs=vmem(7),
        out_specs=vmem(1)[0],
        scratch_shapes=[
            pltpu.VMEM((2, 4 * NST, NST), jnp.bfloat16),
            pltpu.VMEM((5, 8 * NST, 2 * NST), jnp.bfloat16),
        ],
        compiler_params=LIMIT,
        name="beams",
    )(*on_chip(own_steer, col_steer, row_steer, *spectra))


def pack_kernel(a0, a1, a2, a3, rows):
    at = pl.ds(pl.multiple_of(32 * lax.axis_index("win"), 32), 32)
    for s, a in enumerate((a0, a1, a2, a3)):
        for n, block in enumerate(RELAY):
            rows[s, n] = a[block, at, :]


def pack(spectra):
    return pl.pallas_call(
        pack_kernel,
        out_shape=pltpu.VMEM((4, 3, 32, NST), jnp.int16),
        in_specs=vmem(4),
        out_specs=vmem(1)[0],
        compiler_params=LIMIT,
        name="pack",
    )(*on_chip(*spectra))


def fill_columns(sources, f, cols):
    for d in range(4):
        parts = decode(sources, d, f)
        x = jnp.concatenate(parts, axis=0)
        y = jnp.concatenate([q for v in parts for q in (-v[16:32], v[0:16])], axis=0)
        cols[d] = jnp.concatenate([x, y], axis=1)


def emit(parts, cols, r, scratch, ready):
    left = jnp.concatenate(parts, axis=0).T
    for d in range(4):
        cross = jnp.dot(left, cols[d], preferred_element_type=jnp.float32)
        re = cross[:, :NST]
        im = cross[:, NST:]
        inverse = lax.rsqrt(re * re + im * im + 64.0)
        at = pl.ds((r + d) & 3, NST, stride=4)
        scratch[0, at, :] = re * inverse
        scratch[1, at, :] = im * inverse
    ready[0] = scratch[0].astype(jnp.bfloat16)
    ready[1] = scratch[1].astype(jnp.bfloat16)


def block_copy(ready, coherence, offset, sem):
    row = (lax.axis_index("scol") + offset) & 7
    at = pl.ds(pl.multiple_of(row * (4 * NST), 4 * NST), 4 * NST)
    return pltpu.make_async_copy(ready, coherence.at[:, at, :], sem)


def near_kernel(a0, a1, a2, a3, coherence, cols, scratch, ready, sems):
    w, r = lax.axis_index("win"), lax.axis_index("srow")
    sources = (a0, a1, a2, a3)
    fill_columns(sources, w, cols)
    for n, offset in enumerate(ROW_OFF):
        emit(decode(sources, 0 if n == 0 else 3 + n, w), cols, r, scratch, ready.at[n])
        block_copy(ready.at[n], coherence, offset, sems.at[n]).start()
    for n, offset in enumerate(ROW_OFF):
        block_copy(ready.at[n], coherence, offset, sems.at[n]).wait()


def far_kernel(rows, a0, a1, a2, a3, old, coherence, cols, scratch, ready, sems):
    w, r = lax.axis_index("win"), lax.axis_index("srow")
    fill_columns((a0, a1, a2, a3), w, cols)
    for n, offset in enumerate((3, -1, -2)):
        emit(decode([rows.at[k] for k in range(4)], n, 0), cols, r, scratch, ready.at[n])
        block_copy(ready.at[n], coherence, offset, sems.at[n]).start()
    for n, offset in enumerate((3, -1, -2)):
        block_copy(ready.at[n], coherence, offset, sems.at[n]).wait()


def tile_scratch(n):
    return [
        pltpu.VMEM((4, NST, 2 * NST), jnp.bfloat16),
        pltpu.VMEM((2, 4 * NST, NST), jnp.float32),
        pltpu.VMEM((n, 2, 4 * NST, NST), jnp.bfloat16),
        pltpu.SemaphoreType.DMA((n,)),
    ]


TILE = jax.ShapeDtypeStruct((2, 4 * 1024, NST), jnp.bfloat16)
ANY = pl.BlockSpec(memory_space=pl.ANY)


def near_tile(spectra):
    return pl.pallas_call(
        near_kernel,
        in_specs=vmem(4),
        out_specs=ANY,
        scratch_shapes=tile_scratch(5),
        out_shape=TILE,
        compiler_params=LIMIT,
        name="near",
    )(*on_chip(*spectra))


def far_tile(rows, spectra, coherence):
    return pl.pallas_call(
        far_kernel,
        in_specs=vmem(5) + [ANY],
        out_specs=ANY,
        scratch_shapes=tile_scratch(3),
        out_shape=TILE,
        input_output_aliases={5: 0},
        compiler_params=LIMIT,
        name="far",
    )(*on_chip(rows, *spectra), coherence)


def from_offset(value, axis, offset):
    size = lax.axis_size(axis)
    return lax.ppermute(value, axis, [((i + offset) % size, i) for i in range(size)])


def from_partner(value, bit):
    return lax.ppermute(value, "win", [(i ^ bit, i) for i in range(4)])


def body(spectra, bins, travel):
    return local(spectra, bins, travel)


def local(spectra, bins, travel):
    return local(spectra, bins, travel)


def local(spectra, bins, travel):
    payload, scales = pl.pallas_call(
        prep_kernel,
        out_shape=(
            pltpu.VMEM((NPT + 32 * F, NST), jnp.int16),
            pltpu.VMEM((F, 8, NST), jnp.float32),
        ),
        in_specs=[ANY] * 3,
        out_specs=tuple(vmem(2)),
        scratch_shapes=[
            pltpu.VMEM(spectra.shape, jnp.float32),
            pltpu.VMEM(travel.shape, jnp.int32),
            pltpu.SMEM((F,), jnp.int32),
            pltpu.SemaphoreType.DMA((3,)),
        ],
        compiler_params=LIMIT,
        name="prep",
    )(*(pltpu.with_memory_space_constraint(v, pltpu.HBM) for v in (spectra, travel, bins)))
    got = {}
    for axis, offset in SENDS:
        got[axis, offset] = from_offset(payload, axis, offset)
    by_row = [got["srow", d] for d in (1, 2, 3)]
    by_col = [got["scol", d] for d in ROW_OFF[1:]]
    steer0 = steer(scales, [payload])
    steer2 = steer(scales, by_row)
    by_col, steer0, steer2 = lax.optimization_barrier((by_col, steer0, steer2))
    a0 = stack([payload] + by_row + by_col)
    a1 = from_partner(a0, 2)
    steer1 = steer(scales, by_col)
    a0, steer1 = lax.optimization_barrier((a0, steer1))
    a2 = from_partner(a0, 1)
    a1, steer1 = lax.optimization_barrier((a1, steer1))
    a3 = from_partner(a1, 1)
    sources = (a0, a1, a2, a3)
    packed = pack(sources)
    rows = from_offset(packed, "scol", 2)
    partial = beams(steer0, steer1, steer2, sources)
    shares = lax.all_to_all(partial.reshape(128, 4, NST), ALL, 0, 0, tiled=True)
    coherence = far_tile(rows, sources, near_tile(sources))
    beam = shares.astype(jnp.float32).reshape(4, 32, 4, NST).sum(axis=1).reshape(1, 4 * NPT)
    return coherence.reshape(1, 2, 1024, 4, NST), beam


def solution(mesh):
    placed = (P(None, None, "win", ("srow", "scol")), P(), P(("srow", "scol"), "win"))
    return jax.shard_map(
        body,
        mesh=mesh,
        in_specs=placed,
        out_specs=(P("win", None, "srow", None, "scol"), P("win", None)),
        check_vma=False,
    )
```
